512 devices in a mesh: view: 16 (over y, core), row: 4 (over x), col: 8 (over z).
Axes of the slice: x: 4, y: 8, z: 8, core: 2. Of those that a mesh axis runs over, the one named last changes fastest.
Arguments:
- volume: bfloat16 [256, 1024, 1024], P('view', 'row', 'col'), may hold values from -5 to 5
- tf_color: float32 [3, 16], replicated, may hold values from 0 to 1
- tf_opacity: float32 [16], replicated, may hold values from 0.2 to 4
Outputs:
- picture: float32 [4, 16, 64, 1024], P(None, 'view', 'row', 'col')
The draws below stay inside these ranges and needn't reach their ends.
All inputs are finite; a program needn't handle non-finite values.
Results may differ from the reference program's by a relative error of at most 0.00095.
Values may be sent and summed in bfloat16 or wider, within the bound.
A program may use at most 64 MiB of HBM per device.

```python
import math
import jax
import jax.numpy as jnp
from jax import lax

NY = 1024
NX = 1024
KNOTS = 16
NZ = 256
N_VIEW = 16
N_ROW = 4


def levels(own_key, extent, pieces, least, top_value):
    def one(dim, shards_of):
        draws = jax.random.uniform(jax.random.fold_in(jax.random.fold_in(own_key, 6), dim), (shards_of,), jnp.float32, least / len(pieces), top_value / len(pieces))
        return jnp.repeat(jnp.exp(draws), extent[dim] // shards_of).reshape((-1,) + (1,) * (len(extent) - dim - 1))

    level = one(*pieces[0])
    for cut in pieces[1:]:
        level = level * one(*cut)
    return level


def bell_draw(own_key, dims, width, most, pieces=(), kind=jnp.bfloat16):
    values = width * jax.random.normal(own_key, dims, jnp.float32)
    if pieces:
        values = values * levels(own_key, dims, pieces, -0.22, 0.18)
    return jnp.clip(values, -most, most).astype(kind)


def setup_inputs(seed: int = 0) -> dict:
    keys = jax.random.split(jax.random.key(seed), 4)
    return {
        "volume": bell_draw(keys[0], (NZ, NY, NX), 1.0, 5.0, ((0, 16), (1, 4), (2, 8))),
        "tf_color": jnp.clip(jax.random.uniform(keys[1], (3, KNOTS), jnp.float32, 0.0, 1.0), 0.0, 1.0),
        "tf_opacity": jnp.clip(jnp.exp(jax.random.uniform(keys[2], (KNOTS,), jnp.float32, math.log(0.2), math.log(4.0))), 0.2, 4.0),
    }


LIGHT_Z = 0.48
LIGHT_Y = 0.6
LIGHT_X = 0.64
VALUE_LOW = -3.0
VALUE_HIGH = 3.0

def classify(three_slices, tf_color, tf_opacity, depth_total):
    centre = three_slices[1, 1:-1, 1:-1]
    grad_z = (three_slices[2, 1:-1, 1:-1] - three_slices[0, 1:-1, 1:-1]) * 0.5
    grad_y = (three_slices[1, 2:, 1:-1] - three_slices[1, :-2, 1:-1]) * 0.5
    grad_x = (three_slices[1, 1:-1, 2:] - three_slices[1, 1:-1, :-2]) * 0.5
    grad_sq = grad_z * grad_z + grad_y * grad_y + grad_x * grad_x
    shading = 0.35 + 0.65 * jnp.abs(LIGHT_Z * grad_z + LIGHT_Y * grad_y + LIGHT_X * grad_x) / jnp.sqrt(grad_sq + 1.0)
    knot_count = tf_color.shape[1]
    scaled = jnp.clip((centre - VALUE_LOW) * ((knot_count - 1) / (VALUE_HIGH - VALUE_LOW)), 0.0, knot_count - 1.0)
    places = jnp.arange(knot_count, dtype=jnp.float32).reshape(knot_count, 1)
    weights = jnp.maximum(0.0, 1.0 - jnp.abs(scaled.reshape(1, -1) - places))
    colour = jnp.dot(tf_color, weights, precision=lax.Precision.HIGHEST).reshape((3,) + centre.shape)
    extinction = jnp.dot(tf_opacity.reshape(1, knot_count), weights, precision=lax.Precision.HIGHEST).reshape(centre.shape)
    opacity_cell = 1.0 - jnp.exp(-2.0 * extinction * (0.2 + grad_sq / (grad_sq + 1.0)) / depth_total)
    return (colour * shading * opacity_cell, opacity_cell)

def reference(volume, tf_color, tf_opacity):
    slice_count, height, columns = volume.shape
    padded = jnp.pad(volume, 1)

    def advance(running, slice_index):
        colour_sum, through = running
        three_slices = lax.dynamic_slice_in_dim(padded, slice_index, 3, 0).astype(jnp.float32)
        emission, opacity_cell = classify(three_slices, tf_color, tf_opacity, slice_count)
        return ((colour_sum + through * emission, through * (1.0 - opacity_cell)), None)
    initial = (jnp.zeros((3, height, columns), jnp.float32), jnp.ones((height, columns), jnp.float32))
    (colour_sum, through), _ = lax.scan(advance, initial, jnp.arange(slice_count, dtype=jnp.int32))
    whole = jnp.concatenate([colour_sum, (1.0 - through)[None]], axis=0)
    block_rows = NY // (N_VIEW * N_ROW)
    whole = whole.reshape(4, N_ROW, N_VIEW, block_rows, columns).transpose(0, 2, 1, 3, 4)
    return whole.reshape(4, N_VIEW, N_ROW * block_rows, columns)
```

```python
import math

import jax
import jax.numpy as jnp
from jax import lax
from jax.experimental import pallas as pl
from jax.experimental.pallas import tpu as pltpu
from jax.sharding import PartitionSpec as P

LIGHT_Z = 0.48
LIGHT_Y = 0.6
LIGHT_X = 0.64
VALUE_LOW = -3.0
VALUE_HIGH = 3.0
AMBIENT = 0.35
DIFFUSE = 0.65

MESH = pl.DeviceIdType.MESH
LANES = 128
STRIP = 16
HALF = 8


def tables_of(color_ref, opacity_ref, knots, opacity_scale):
    lane = lax.broadcasted_iota(jnp.int32, (HALF, LANES), 1)
    place = lane.astype(jnp.float32)
    pairs = []
    for channel in range(4):
        values = jnp.zeros((HALF, LANES), jnp.float32)
        for k in range(knots):
            entry = color_ref[channel, k] if channel < 3 else opacity_ref[k] * opacity_scale
            values = jnp.where(lane == k, entry, values)
        slope = pltpu.roll(values, LANES - 1, 1) - values
        slope = jnp.where(lane < knots - 1, slope, 0.0)
        pairs.append((values - place * slope, slope))
    return pairs


def look_up(table, index):
    return jnp.take_along_axis(table, index, axis=1, mode="promise_in_bounds")


def kernel(
    counts,
    volume,
    color_ref,
    opacity_ref,
    out_ref,
    cells,
    edges,
    edges_left,
    edges_right,
    across,
    picked,
    outgoing,
    arrived,
    load_sem,
    halo_send,
    halo_recv,
    part_send,
    part_recv,
):
    views, rows, cols = counts
    depth, height, _ = volume.shape
    knots = color_ref.shape[1]
    v, r, c = lax.axis_index("view"), lax.axis_index("row"), lax.axis_index("col")
    body = pl.ds(STRIP, height)

    load = pltpu.make_async_copy(volume, cells.at[pl.ds(1, depth), body], load_sem)
    load.start()

    barrier = pltpu.get_barrier_semaphore()
    for step in range(1, views):
        pl.semaphore_signal(barrier, inc=1, device_id={"view": lax.rem(v + step, views)}, device_id_type=MESH)
    beside = [
        (v > 0, {"view": v - 1}),
        (v < views - 1, {"view": v + 1}),
        (r > 0, {"row": r - 1}),
        (r < rows - 1, {"row": r + 1}),
        (c > 0, {"col": c - 1}),
        (c < cols - 1, {"col": c + 1}),
    ]
    for there, where in beside[2:]:

        @pl.when(there)
        def _():
            pl.semaphore_signal(barrier, inc=1, device_id=where, device_id_type=MESH)

    expected = views - 1
    for there, _ in beside[2:]:
        expected = expected + there.astype(jnp.int32)
    pl.semaphore_wait(barrier, expected)

    sources = [
        volume.at[pl.ds(0, 1)],
        volume.at[pl.ds(depth - 1, 1)],
        volume.at[:, pl.ds(0, STRIP)],
        volume.at[:, pl.ds(height - STRIP, STRIP)],
        edges,
        edges,
    ]
    landings = [
        cells.at[pl.ds(depth + 1, 1), body],
        cells.at[pl.ds(0, 1), body],
        cells.at[pl.ds(1, depth), pl.ds(STRIP + height, STRIP)],
        cells.at[pl.ds(1, depth), pl.ds(0, STRIP)],
        edges_right,
        edges_left,
    ]
    copies = [
        pltpu.make_async_remote_copy(
            src_ref=sources[i],
            dst_ref=landings[i],
            send_sem=halo_send.at[i],
            recv_sem=halo_recv.at[i],
            device_id=beside[i][1],
            device_id_type=MESH,
        )
        for i in range(6)
    ]
    for i in range(4):

        @pl.when(beside[i][0])
        def _():
            copies[i].start()

    for i in range(6):

        @pl.when(jnp.logical_not(beside[i ^ 1][0]))
        def _():
            landings[i][...] = jnp.zeros(landings[i].shape, landings[i].dtype)

    tables = tables_of(color_ref, opacity_ref, knots, -8.0 * math.log2(math.e) / (depth * views))

    k = lax.broadcasted_iota(jnp.int32, (2 * LANES, LANES), 0)
    n = lax.broadcasted_iota(jnp.int32, (2 * LANES, LANES), 1)
    beyond = k - LANES
    plus = ((k < LANES) & (k == n + 1)) | ((beyond >= depth) & (beyond < 2 * depth) & (n == LANES - 1))
    minus = ((k < LANES) & (k == n - 1)) | ((beyond >= 0) & (beyond < depth) & (n == 0))
    across[...] = (plus.astype(jnp.float32) - minus.astype(jnp.float32)).astype(jnp.bfloat16)
    z_of = lax.broadcasted_iota(jnp.int32, (depth, STRIP, LANES), 0)
    lane_of = lax.broadcasted_iota(jnp.int32, (depth, STRIP, LANES), 2)
    own = (lane_of == z_of) | (lane_of == z_of + depth)
    picked[...] = own.astype(jnp.float32).astype(jnp.bfloat16)

    load.wait()

    lane = lax.broadcasted_iota(jnp.int32, (STRIP, LANES), 1)

    def gather_edges(s, carry):
        packed = jnp.zeros((STRIP, LANES), jnp.float32)
        at = pl.ds(pl.multiple_of(STRIP + s * STRIP, STRIP), STRIP)
        for z in range(depth):
            row = cells[1 + z, at].astype(jnp.float32)
            packed = jnp.where(lane == z, pltpu.roll(row, z + 1, 1), packed)
            packed = jnp.where(lane == depth + z, pltpu.roll(row, depth + z, 1), packed)
        edges[pl.ds(pl.multiple_of(s * STRIP, STRIP), STRIP)] = packed.astype(jnp.bfloat16)
        return carry

    lax.fori_loop(0, height // STRIP, gather_edges, 0)
    for i in range(4, 6):

        @pl.when(beside[i][0])
        def _():
            copies[i].start()

    for i in range(6):

        @pl.when(beside[i ^ 1][0])
        def _():
            copies[i].wait_recv()

    def partial_image(s):
        window = pl.ds(pl.multiple_of(s * STRIP, STRIP), 3 * STRIP)
        inner = pl.ds(pl.multiple_of(s * STRIP + STRIP, STRIP), STRIP)
        at = pl.ds(pl.multiple_of(s * STRIP, STRIP), STRIP)
        outside = jnp.where(lane < depth, edges_left[at].astype(jnp.float32), edges_right[at].astype(jnp.float32))
        outside = outside.astype(jnp.bfloat16)[None] * picked[...]
        middle = cells[pl.ds(1, depth), inner]
        left_hand = jnp.concatenate(
            [middle.reshape(depth * STRIP, LANES), outside.reshape(depth * STRIP, LANES)], axis=1
        )
        diff_x = jnp.dot(left_hand, across[...], preferred_element_type=jnp.float32)
        colour = [[jnp.zeros((HALF, LANES), jnp.float32)] * 3 for _ in range(2)]
        through = [jnp.ones((HALF, LANES), jnp.float32) for _ in range(2)]
        behind = cells[0, inner].astype(jnp.float32)
        here = cells[1, window].astype(jnp.float32)
        for z in range(depth):
            if z + 1 < depth:
                ahead_rows = cells[z + 2, window].astype(jnp.float32)
                ahead = ahead_rows[STRIP : 2 * STRIP]
            else:
                ahead_rows = None
                ahead = cells[z + 2, inner].astype(jnp.float32)
            near = here[HALF : 5 * HALF]
            diff_y = pltpu.roll(near, 4 * HALF - 1, 0) - pltpu.roll(near, 1, 0)
            diff_y = diff_y[HALF : 3 * HALF]
            centre_rows = here[STRIP : 2 * STRIP]
            diff_z = ahead - behind
            for h in range(2):
                part = slice(h * HALF, (h + 1) * HALF)
                gz, gy = diff_z[part], diff_y[part]
                gx = diff_x[z * STRIP + h * HALF : z * STRIP + (h + 1) * HALF]
                value = centre_rows[part]
                root = lax.rsqrt(gz * gz + gy * gy + gx * gx + 4.0)
                lit = jnp.abs(DIFFUSE * LIGHT_Z * gz + DIFFUSE * LIGHT_Y * gy + DIFFUSE * LIGHT_X * gx)
                shading = AMBIENT + lit * root
                scale = (knots - 1) / (VALUE_HIGH - VALUE_LOW)
                scaled = jnp.clip(value * scale - VALUE_LOW * scale, 0.0, knots - 1.0)
                index = scaled.astype(jnp.int32)
                red, green, blue, extinction = [
                    look_up(base, index) + look_up(slope, index) * scaled for base, slope in tables
                ]
                passed = jnp.exp2(extinction * (0.3 - root * root))
                after = through[h] * passed
                weight = (through[h] - after) * shading
                through[h] = after
                for channel, value_of in enumerate((red, green, blue)):
                    colour[h][channel] = colour[h][channel] + value_of * weight
            behind, here = centre_rows, ahead_rows
        return [
            jnp.concatenate([colour[0][0], colour[1][0]], axis=0),
            jnp.concatenate([colour[0][1], colour[1][1]], axis=0),
            jnp.concatenate([colour[0][2], colour[1][2]], axis=0),
            1.0 - jnp.concatenate(through, axis=0),
        ]

    def send_to(s):
        return pltpu.make_async_remote_copy(
            src_ref=outgoing.at[s],
            dst_ref=arrived.at[v],
            send_sem=part_send.at[s],
            recv_sem=part_recv.at[v],
            device_id={"view": s},
            device_id_type=MESH,
        )

    def work(step, carry):
        offset = jnp.where(step % 2 == 0, views // 2 - step // 2, views // 2 + (step + 1) // 2)
        s = lax.rem(v + offset, views)
        image = partial_image(s)
        for channel in range(4):
            outgoing[s, channel] = image[channel].astype(jnp.bfloat16)

        @pl.when(s != v)
        def _():
            send_to(s).start()

        return carry

    lax.fori_loop(0, views, work, 0)

    for i in range(6):

        @pl.when(beside[i][0])
        def _():
            copies[i].wait_send()

    arrived[v] = outgoing[v]
    image = [jnp.zeros((STRIP, LANES), jnp.float32)] * 3
    through = jnp.ones((STRIP, LANES), jnp.float32)
    for source in range(views):

        @pl.when(v != source)
        def _():
            pltpu.make_async_remote_copy(
                src_ref=outgoing.at[source],
                dst_ref=arrived.at[source],
                send_sem=part_send.at[source],
                recv_sem=part_recv.at[source],
                device_id={"view": source},
                device_id_type=MESH,
            ).wait()

        layer = arrived[source].astype(jnp.float32)
        for channel in range(3):
            image[channel] = image[channel] + through * layer[channel]
        through = through * (1.0 - layer[3])
    for channel in range(3):
        out_ref[channel, 0] = image[channel]
    out_ref[3, 0] = 1.0 - through


def solution(mesh):
    counts = tuple(mesh.shape[axis] for axis in ("view", "row", "col"))

    def on_device(volume, tf_color, tf_opacity):
        depth, height, width = volume.shape
        views = counts[0]
        half = jnp.bfloat16
        return pl.pallas_call(
            lambda *refs: kernel(counts, *refs),
            name="render",
            out_shape=jax.ShapeDtypeStruct((4, 1, height // views, width), jnp.float32),
            in_specs=[
                pl.BlockSpec(memory_space=pl.ANY),
                pl.BlockSpec(memory_space=pltpu.SMEM),
                pl.BlockSpec(memory_space=pltpu.SMEM),
            ],
            out_specs=pl.BlockSpec(memory_space=pltpu.VMEM),
            scratch_shapes=[
                pltpu.VMEM((depth + 2, height + 2 * STRIP, width), half),
                pltpu.VMEM((height, width), half),
                pltpu.VMEM((height, width), half),
                pltpu.VMEM((height, width), half),
                pltpu.VMEM((2 * width, width), half),
                pltpu.VMEM((depth, STRIP, width), half),
                pltpu.VMEM((views, 4, STRIP, width), half),
                pltpu.VMEM((views, 4, STRIP, width), half),
                pltpu.SemaphoreType.DMA,
                pltpu.SemaphoreType.DMA((6,)),
                pltpu.SemaphoreType.DMA((6,)),
                pltpu.SemaphoreType.DMA((views,)),
                pltpu.SemaphoreType.DMA((views,)),
            ],
            compiler_params=pltpu.CompilerParams(collective_id=0, has_side_effects=True),
        )(volume, tf_color, tf_opacity)

    return jax.shard_map(
        on_device,
        mesh=mesh,
        in_specs=(P("view", "row", "col"), P(), P()),
        out_specs=P(None, "view", "row", "col"),
        check_vma=False,
    )
```

```python
import math

import jax
import jax.numpy as jnp
from jax import lax
from jax.experimental import pallas as pl
from jax.experimental.pallas import tpu as pltpu
from jax.sharding import PartitionSpec as P

LIGHT_Z = 0.48
LIGHT_Y = 0.6
LIGHT_X = 0.64
VALUE_LOW = -3.0
VALUE_HIGH = 3.0
AMBIENT = 0.35
DIFFUSE = 0.65

MESH = pl.DeviceIdType.MESH
LANES = 128
STRIP = 16
HALF = 8
CORES = 2


def tables_of(color_ref, opacity_ref, knots, scales):
    row = lax.broadcasted_iota(jnp.int32, (HALF, LANES), 0)
    lane = lax.broadcasted_iota(jnp.int32, (HALF, LANES), 1)
    pairs = []
    for channel in range(4):
        at_knot = [
            (color_ref[channel, k] if channel < 3 else opacity_ref[k]) * scales[channel] for k in range(knots)
        ]
        odd = jnp.zeros((HALF, LANES), jnp.float32)
        slope = jnp.zeros((HALF, LANES), jnp.float32)
        for k in range(1, knots, 2):
            odd = jnp.where(row == k // 2, at_knot[k], odd)
        for k in range(knots - 1):
            slope = jnp.where(lane == k, at_knot[k + 1] - at_knot[k], slope)
        pairs.append((odd, slope))
    return pairs


def look_up(table, index, axis):
    other = 1 - axis
    dims = lax.GatherDimensionNumbers(
        offset_dims=(),
        collapsed_slice_dims=(axis,),
        start_index_map=(axis,),
        operand_batching_dims=(other,),
        start_indices_batching_dims=(other,),
    )
    mode = lax.GatherScatterMode.PROMISE_IN_BOUNDS
    return lax.gather(table, index[..., None], dims, slice_sizes=(1, 1), mode=mode)


def kernel(
    counts,
    volume,
    color_ref,
    opacity_ref,
    out_ref,
    cells,
    wide,
    edges,
    edges_left,
    edges_right,
    across,
    picked,
    parts,
    theirs,
    outgoing,
    arrived,
    load_sem,
    halo_send,
    halo_recv,
    swap_send,
    swap_recv,
    part_send,
    part_recv,
):
    views, rows, cols = counts
    chips = views // CORES
    depth, height, _ = volume.shape
    knots = color_ref.shape[1]
    groups = LANES // (2 * depth)
    group_rows = height // groups
    v, r, c = lax.axis_index("view"), lax.axis_index("row"), lax.axis_index("col")
    core, chip = lax.rem(v, CORES), v // CORES
    partner = v + 1 - 2 * core
    body = pl.ds(STRIP, height)

    load = pltpu.make_async_copy(volume, cells.at[pl.ds(1, depth), body], load_sem)
    load.start()

    beside = [
        (v > 0, {"view": v - 1}),
        (v < views - 1, {"view": v + 1}),
        (r > 0, {"row": r - 1}),
        (r < rows - 1, {"row": r + 1}),
        (c > 0, {"col": c - 1}),
        (c < cols - 1, {"col": c + 1}),
    ]
    barrier = pltpu.get_barrier_semaphore()
    expected = chips - 1
    for there, where in beside:
        expected = expected + there.astype(jnp.int32)

        @pl.when(there)
        def _():
            pl.semaphore_signal(barrier, inc=1, device_id=where, device_id_type=MESH)

    for step in range(1, chips):
        other = lax.rem(v + CORES * step, views)
        pl.semaphore_signal(barrier, inc=1, device_id={"view": other}, device_id_type=MESH)

    group_of = lax.broadcasted_iota(jnp.int32, (groups * depth, STRIP, LANES), 0)
    lane_of = lax.broadcasted_iota(jnp.int32, (groups * depth, STRIP, LANES), 2)
    first_lane = group_of + (group_of // depth) * depth
    own = (lane_of == first_lane) | (lane_of == first_lane + depth)
    picked[...] = own.astype(jnp.float32).astype(jnp.bfloat16)

    pl.semaphore_wait(barrier, expected)

    sources = [
        volume.at[pl.ds(0, 1)],
        volume.at[pl.ds(depth - 1, 1)],
        volume.at[:, pl.ds(0, STRIP)],
        volume.at[:, pl.ds(height - STRIP, STRIP)],
        edges,
        edges,
    ]
    landings = [
        cells.at[pl.ds(depth + 1, 1), body],
        cells.at[pl.ds(0, 1), body],
        cells.at[pl.ds(1, depth), pl.ds(STRIP + height, STRIP)],
        cells.at[pl.ds(1, depth), pl.ds(0, STRIP)],
        edges_right,
        edges_left,
    ]
    copies = [
        pltpu.make_async_remote_copy(
            src_ref=sources[i],
            dst_ref=landings[i],
            send_sem=halo_send.at[i],
            recv_sem=halo_recv.at[i],
            device_id=beside[i][1],
            device_id_type=MESH,
        )
        for i in range(6)
    ]
    for i in range(4):

        @pl.when(beside[i][0])
        def _():
            copies[i].start()

    load.wait()

    narrow = lax.broadcasted_iota(jnp.int32, (STRIP, LANES), 1)
    from_left = (narrow & (2 * depth - 1)) < depth
    taken = jnp.where(from_left, LANES - 1, 0).astype(jnp.int16)
    for b in range(group_rows // STRIP):
        packed = jnp.zeros((STRIP, LANES), jnp.bfloat16)
        for g in range(groups):
            for z in range(depth):
                row = cells[1 + z, pl.ds(STRIP + g * group_rows + b * STRIP, STRIP)]
                packed = packed + look_up(row, taken, 1) * picked[g * depth + z]
        edges[pl.ds(b * STRIP, STRIP)] = packed
    for i in range(4, 6):

        @pl.when(beside[i][0])
        def _():
            copies[i].start()

    for i in range(6):

        @pl.when(jnp.logical_not(beside[i ^ 1][0]))
        def _():
            landings[i][...] = jnp.zeros(landings[i].shape, landings[i].dtype)

    light = DIFFUSE * LIGHT_Z
    scales = [light] * 3 + [-8.0 * math.log2(math.e) / (depth * views)]
    tables = tables_of(color_ref, opacity_ref, knots, scales)

    k = lax.broadcasted_iota(jnp.int32, (2 * LANES, LANES), 0)
    n = lax.broadcasted_iota(jnp.int32, (2 * LANES, LANES), 1)
    inside = k < LANES
    place = k & (2 * depth - 1)
    plus = (inside & (k == n + 1)) | ((k >= LANES) & (place >= depth) & (n == LANES - 1))
    minus = (inside & (k == n - 1)) | ((k >= LANES) & (place < depth) & (n == 0))
    across[...] = (plus.astype(jnp.float32) - minus.astype(jnp.float32)).astype(jnp.bfloat16)

    def widen(s, carry):
        for z in range(depth):
            some = cells[1 + z, pl.ds(pl.multiple_of(STRIP + s * STRIP, STRIP), STRIP)]
            wide[z, pl.ds(pl.multiple_of(HALF + s * STRIP, HALF), STRIP)] = some.astype(jnp.float32)
        return carry

    lax.fori_loop(0, height // STRIP, widen, 0)

    for i in range(6):

        @pl.when(beside[i ^ 1][0])
        def _():
            copies[i].wait_recv()

    for z in range(depth):
        wide[z, pl.ds(0, HALF)] = cells[1 + z, pl.ds(0, STRIP)].astype(jnp.float32)[HALF:]
        wide[z, pl.ds(HALF + height, HALF)] = cells[1 + z, pl.ds(STRIP + height, STRIP)].astype(jnp.float32)[:HALF]

    def partial_image(s):
        inner = pl.ds(pl.multiple_of(s * STRIP + STRIP, STRIP), STRIP)
        b = pl.ds(pl.multiple_of(lax.rem(s * STRIP, group_rows), STRIP), STRIP)
        outside = jnp.where(from_left, edges_left[b].astype(jnp.float32), edges_right[b].astype(jnp.float32))
        mine = picked[pl.ds((s * STRIP // group_rows) * depth, depth)]
        outside = outside.astype(jnp.bfloat16)[None] * mine
        middle = cells[pl.ds(1, depth), inner]
        left_hand = jnp.concatenate(
            [middle.reshape(depth * STRIP, LANES), outside.reshape(depth * STRIP, LANES)], axis=1
        )
        diff_x = jnp.dot(left_hand, across[...], preferred_element_type=jnp.float32)
        colour = [[jnp.zeros((HALF, LANES), jnp.float32)] * 3 for _ in range(2)]
        through = [jnp.ones((HALF, LANES), jnp.float32) for _ in range(2)]
        first = cells[0, inner].astype(jnp.float32)
        last = cells[depth + 1, inner].astype(jnp.float32)
        for z in range(depth):
            for h in range(2):
                base = pl.multiple_of(s * STRIP, STRIP) + h * HALF
                part = slice(h * HALF, (h + 1) * HALF)
                here = pl.ds(base + HALF, HALF)
                value = wide[z, here]
                behind = wide[z - 1, here] if z > 0 else first[part]
                ahead = wide[z + 1, here] if z + 1 < depth else last[part]
                gz = ahead - behind
                gy = wide[z, pl.ds(base + HALF + 1, HALF)] - wide[z, pl.ds(base + HALF - 1, HALF)]
                gx = diff_x[z * STRIP + h * HALF : z * STRIP + (h + 1) * HALF]
                root = lax.rsqrt(gz * gz + gy * gy + (gx * gx + 4.0))
                lit = jnp.abs(gz + (LIGHT_Y / LIGHT_Z) * gy + (LIGHT_X / LIGHT_Z) * gx)
                shading = AMBIENT / light + lit * root
                scale = (knots - 1) / (VALUE_HIGH - VALUE_LOW)
                scaled = jnp.clip(value * scale - VALUE_LOW * scale, 0.0, knots - 1.0)
                interval = scaled.astype(jnp.int32)
                pair = lax.shift_right_logical(interval, 1)
                away = scaled - (interval | 1).astype(jnp.float32)
                red, green, blue, extinction = [
                    look_up(odd, pair, 0) + look_up(slope, interval, 1) * away for odd, slope in tables
                ]
                passed = jnp.exp2(extinction * (0.3 - root * root))
                after = through[h] * passed
                weight = (through[h] - after) * shading
                through[h] = after
                for channel, value_of in enumerate((red, green, blue)):
                    colour[h][channel] = colour[h][channel] + value_of * weight
        return [jnp.concatenate([colour[0][i], colour[1][i]], axis=0) for i in range(3)] + [
            jnp.concatenate(through, axis=0)
        ]

    def chip_of(i):
        ahead = jnp.where(i % 2 == 0, chips // 2 - i // 2, chips // 2 + (i + 1) // 2)
        return lax.rem(chip + ahead, chips)

    def swap(i):
        return pltpu.make_async_remote_copy(
            src_ref=parts.at[i],
            dst_ref=theirs.at[i],
            send_sem=swap_send.at[i],
            recv_sem=swap_recv.at[i],
            device_id={"view": partner},
            device_id_type=MESH,
        )

    def hand_over(to_chip, from_chip):
        return pltpu.make_async_remote_copy(
            src_ref=outgoing.at[to_chip],
            dst_ref=arrived.at[from_chip],
            send_sem=part_send.at[to_chip],
            recv_sem=part_recv.at[from_chip],
            device_id={"view": CORES * to_chip + core},
            device_id_type=MESH,
        )

    def work(step, carry):
        i = lax.rem(step, chips)
        late = step // chips
        to_chip = chip_of(i)
        s = CORES * to_chip + jnp.where(late == 1, core, 1 - core)
        image = partial_image(s)
        for channel in range(4):
            parts[step, channel] = image[channel]

        @pl.when(late == 0)
        def _():
            swap(i).start()

        @pl.when(late == 1)
        def _():
            swap(i).wait_recv()
            front, back = [], []
            for channel in range(4):
                a, b = parts[step, channel], theirs[i, channel]
                front.append(jnp.where(core == 0, a, b))
                back.append(jnp.where(core == 0, b, a))
            for channel in range(3):
                outgoing[to_chip, channel] = (front[channel] + front[3] * back[channel]).astype(jnp.bfloat16)
            outgoing[to_chip, 3] = (1.0 - front[3] * back[3]).astype(jnp.bfloat16)

            @pl.when(to_chip != chip)
            def _():
                hand_over(to_chip, chip).start()

        return carry

    lax.fori_loop(0, views, work, 0)

    for i in range(6):

        @pl.when(beside[i][0])
        def _():
            copies[i].wait_send()

    for i in range(chips):
        swap(i).wait_send()

    arrived[chip] = outgoing[chip]
    image = [jnp.zeros((STRIP, LANES), jnp.float32)] * 3
    through = jnp.ones((STRIP, LANES), jnp.float32)
    for source in range(chips):

        @pl.when(chip != source)
        def _():
            hand_over(source, source).wait()

        layer = arrived[source].astype(jnp.float32)
        for channel in range(3):
            image[channel] = image[channel] + through * layer[channel]
        through = through * (1.0 - layer[3])
    for channel in range(3):
        out_ref[channel, 0] = image[channel]
    out_ref[3, 0] = 1.0 - through


def solution(mesh):
    counts = tuple(mesh.shape[axis] for axis in ("view", "row", "col"))

    def on_device(volume, tf_color, tf_opacity):
        depth, height, width = volume.shape
        views = counts[0]
        chips = views // CORES
        half, full = jnp.bfloat16, jnp.float32
        edge_rows = height * 2 * depth // LANES
        return pl.pallas_call(
            lambda *refs: kernel(counts, *refs),
            name="render",
            out_shape=jax.ShapeDtypeStruct((4, 1, height // views, width), jnp.float32),
            in_specs=[
                pl.BlockSpec(memory_space=pltpu.HBM),
                pl.BlockSpec(memory_space=pltpu.SMEM),
                pl.BlockSpec(memory_space=pltpu.SMEM),
            ],
            out_specs=pl.BlockSpec(memory_space=pltpu.VMEM),
            scratch_shapes=[
                pltpu.VMEM((depth + 2, height + 2 * STRIP, width), half),
                pltpu.VMEM((depth, height + 2 * HALF, width), full),
                pltpu.VMEM((edge_rows, width), half),
                pltpu.VMEM((edge_rows, width), half),
                pltpu.VMEM((edge_rows, width), half),
                pltpu.VMEM((2 * width, width), half),
                pltpu.VMEM((LANES // 2, STRIP, width), half),
                pltpu.VMEM((views, 4, STRIP, width), full),
                pltpu.VMEM((chips, 4, STRIP, width), full),
                pltpu.VMEM((chips, 4, STRIP, width), half),
                pltpu.VMEM((chips, 4, STRIP, width), half),
                pltpu.SemaphoreType.DMA,
                pltpu.SemaphoreType.DMA((6,)),
                pltpu.SemaphoreType.DMA((6,)),
                pltpu.SemaphoreType.DMA((chips,)),
                pltpu.SemaphoreType.DMA((chips,)),
                pltpu.SemaphoreType.DMA((chips,)),
                pltpu.SemaphoreType.DMA((chips,)),
            ],
            compiler_params=pltpu.CompilerParams(collective_id=0, has_side_effects=True),
        )(volume, tf_color, tf_opacity)

    return jax.shard_map(
        on_device,
        mesh=mesh,
        in_specs=(P("view", "row", "col"), P(), P()),
        out_specs=P(None, "view", "row", "col"),
        check_vma=False,
    )
```

```python
import math

import jax
import jax.numpy as jnp
from jax import lax
from jax.experimental import pallas as pl
from jax.experimental.pallas import tpu as pltpu
from jax.sharding import PartitionSpec as P

LIGHT_Z = 0.48
LIGHT_Y = 0.6
LIGHT_X = 0.64
VALUE_LOW = -3.0
VALUE_HIGH = 3.0
AMBIENT = 0.35
DIFFUSE = 0.65

MESH = pl.DeviceIdType.MESH
LANES = 128
STRIP = 16
HALF = 8
CORES = 2


def tables_of(color_ref, opacity_ref, knots, scales):
    row = lax.broadcasted_iota(jnp.int32, (HALF, LANES), 0)
    lane = lax.broadcasted_iota(jnp.int32, (HALF, LANES), 1)
    pairs = []
    for channel in range(4):
        at_knot = [
            (color_ref[channel, k] if channel < 3 else opacity_ref[k]) * scales[channel] for k in range(knots)
        ]
        odd = jnp.zeros((HALF, LANES), jnp.float32)
        slope = jnp.zeros((HALF, LANES), jnp.float32)
        for k in range(1, knots, 2):
            odd = jnp.where(row == k // 2, at_knot[k], odd)
        for k in range(knots - 1):
            slope = jnp.where(lane == k, at_knot[k + 1] - at_knot[k], slope)
        pairs.append((odd, slope))
    return pairs


def look_up(table, index, axis):
    other = 1 - axis
    dims = lax.GatherDimensionNumbers(
        offset_dims=(),
        collapsed_slice_dims=(axis,),
        start_index_map=(axis,),
        operand_batching_dims=(other,),
        start_indices_batching_dims=(other,),
    )
    mode = lax.GatherScatterMode.PROMISE_IN_BOUNDS
    return lax.gather(table, index[..., None], dims, slice_sizes=(1, 1), mode=mode)


def kernel(
    counts,
    volume,
    color_hbm,
    opacity_hbm,
    out_ref,
    color_ref,
    opacity_ref,
    cells,
    wide,
    edges,
    edges_left,
    edges_right,
    across,
    diff_even,
    diff_odd,
    picked,
    parts,
    theirs,
    outgoing,
    arrived,
    load_sem,
    table_sem,
    ready_sem,
    halo_send,
    halo_recv,
    swap_send,
    swap_recv,
    part_send,
    part_recv,
):
    views, rows, cols = counts
    chips = views // CORES
    depth, height, _ = volume.shape
    knots = color_ref.shape[1]
    groups = LANES // (2 * depth)
    group_rows = height // groups
    v, r, c = lax.axis_index("view"), lax.axis_index("row"), lax.axis_index("col")
    core, chip = lax.rem(v, CORES), v // CORES
    partner = v + 1 - 2 * core
    body = pl.ds(STRIP, height)

    load = pltpu.make_async_copy(volume, cells.at[pl.ds(1, depth), body], load_sem)
    load.start()
    loads = [
        pltpu.make_async_copy(color_hbm, color_ref, table_sem.at[0]),
        pltpu.make_async_copy(opacity_hbm, opacity_ref, table_sem.at[1]),
    ]
    for one in loads:
        one.start()

    beside = [
        (v > 0, {"view": v - 1}),
        (v < views - 1, {"view": v + 1}),
        (r > 0, {"row": r - 1}),
        (r < rows - 1, {"row": r + 1}),
        (c > 0, {"col": c - 1}),
        (c < cols - 1, {"col": c + 1}),
    ]
    barrier = pltpu.get_barrier_semaphore()
    expected = 0
    for there, where in beside:
        expected = expected + there.astype(jnp.int32)

        @pl.when(there)
        def _():
            pl.semaphore_signal(barrier, inc=1, device_id=where, device_id_type=MESH)

    def greet(semaphore, distance):
        for way in sorted({distance, chips - distance}):
            other = lax.rem(v + CORES * way, views)
            pl.semaphore_signal(semaphore, inc=1, device_id={"view": other}, device_id_type=MESH)
        return len({distance, chips - distance})

    expected = expected + greet(barrier, 1)

    group_of = lax.broadcasted_iota(jnp.int32, (groups * depth, STRIP, LANES), 0)
    lane_of = lax.broadcasted_iota(jnp.int32, (groups * depth, STRIP, LANES), 2)
    first_lane = group_of + (group_of // depth) * depth
    own = (lane_of == first_lane) | (lane_of == first_lane + depth)
    picked[...] = own.astype(jnp.float32).astype(jnp.bfloat16)

    pl.semaphore_wait(barrier, expected)

    sources = [
        volume.at[pl.ds(0, 1)],
        volume.at[pl.ds(depth - 1, 1)],
        volume.at[:, pl.ds(0, STRIP)],
        volume.at[:, pl.ds(height - STRIP, STRIP)],
        edges,
        edges,
    ]
    landings = [
        cells.at[pl.ds(depth + 1, 1), body],
        cells.at[pl.ds(0, 1), body],
        cells.at[pl.ds(1, depth), pl.ds(STRIP + height, STRIP)],
        cells.at[pl.ds(1, depth), pl.ds(0, STRIP)],
        edges_right,
        edges_left,
    ]
    copies = [
        pltpu.make_async_remote_copy(
            src_ref=sources[i],
            dst_ref=landings[i],
            send_sem=halo_send.at[i],
            recv_sem=halo_recv.at[i],
            device_id=beside[i][1],
            device_id_type=MESH,
        )
        for i in range(6)
    ]
    for i in range(4):

        @pl.when(beside[i][0])
        def _():
            copies[i].start()

    rounds = max(chips // 2 - 1, 0).bit_length()
    heard = [greet(ready_sem.at[0], 1)] if rounds > 0 else []

    load.wait()

    narrow = lax.broadcasted_iota(jnp.int32, (STRIP, LANES), 1)
    from_left = (narrow & (2 * depth - 1)) < depth
    taken = jnp.where(from_left, LANES - 1, 0).astype(jnp.int16)
    for b in range(group_rows // STRIP):
        packed = jnp.zeros((STRIP, LANES), jnp.bfloat16)
        for g in range(groups):
            for z in range(depth):
                row = cells[1 + z, pl.ds(STRIP + g * group_rows + b * STRIP, STRIP)]
                packed = packed + look_up(row, taken, 1) * picked[g * depth + z]
        edges[pl.ds(b * STRIP, STRIP)] = packed
    for i in range(4, 6):

        @pl.when(beside[i][0])
        def _():
            copies[i].start()

    for k in range(1, rounds):
        pl.semaphore_wait(ready_sem.at[k - 1], heard[-1])
        heard.append(greet(ready_sem.at[k], 2**k))

    for i in range(6):

        @pl.when(jnp.logical_not(beside[i ^ 1][0]))
        def _():
            landings[i][...] = jnp.zeros(landings[i].shape, landings[i].dtype)

    scale = (knots - 1) / (VALUE_HIGH - VALUE_LOW)
    square = (2.0 * scale) ** 2
    light = DIFFUSE * LIGHT_Z
    scales = [light] * 3 + [-2.0 * square * math.log2(math.e) / (depth * views)]

    def placed(some):
        return some.astype(jnp.float32) * scale - VALUE_LOW * scale

    for one in loads:
        one.wait()
    tables = tables_of(color_ref, opacity_ref, knots, scales)

    k = lax.broadcasted_iota(jnp.int32, (2 * LANES, LANES), 0)
    n = lax.broadcasted_iota(jnp.int32, (2 * LANES, LANES), 1)
    inside = k < LANES
    place = k & (2 * depth - 1)
    plus = (inside & (k == n + 1)) | ((k >= LANES) & (place >= depth) & (n == LANES - 1))
    minus = (inside & (k == n - 1)) | ((k >= LANES) & (place < depth) & (n == 0))
    across[...] = ((plus.astype(jnp.float32) - minus.astype(jnp.float32)) * scale).astype(jnp.bfloat16)

    def widen(s, carry):
        for z in range(depth):
            some = cells[1 + z, pl.ds(pl.multiple_of(STRIP + s * STRIP, STRIP), STRIP)]
            wide[z, pl.ds(pl.multiple_of(HALF + s * STRIP, HALF), STRIP)] = placed(some)
        return carry

    lax.fori_loop(0, height // STRIP, widen, 0)

    for i in range(6):

        @pl.when(beside[i ^ 1][0])
        def _():
            copies[i].wait_recv()

    for z in range(depth):
        wide[z, pl.ds(0, HALF)] = placed(cells[1 + z, pl.ds(0, STRIP)])[HALF:]
        wide[z, pl.ds(HALF + height, HALF)] = placed(cells[1 + z, pl.ds(STRIP + height, STRIP)])[:HALF]
    if rounds > 0:
        pl.semaphore_wait(ready_sem.at[rounds - 1], heard[-1])

    def difference_x(s):
        inner = pl.ds(pl.multiple_of(s * STRIP + STRIP, STRIP), STRIP)
        b = pl.ds(pl.multiple_of(lax.rem(s * STRIP, group_rows), STRIP), STRIP)
        outside = jnp.where(from_left, edges_left[b].astype(jnp.float32), edges_right[b].astype(jnp.float32))
        mine = picked[pl.ds((s * STRIP // group_rows) * depth, depth)]
        outside = outside.astype(jnp.bfloat16)[None] * mine
        middle = cells[pl.ds(1, depth), inner]
        left_hand = jnp.concatenate(
            [middle.reshape(depth * STRIP, LANES), outside.reshape(depth * STRIP, LANES)], axis=1
        )
        return jnp.dot(left_hand, across[...], preferred_element_type=jnp.float32)

    def partial_image(s, diff):
        inner = pl.ds(pl.multiple_of(s * STRIP + STRIP, STRIP), STRIP)
        colour = [[jnp.zeros((HALF, LANES), jnp.float32)] * 3 for _ in range(2)]
        through = [jnp.ones((HALF, LANES), jnp.float32) for _ in range(2)]
        first = placed(cells[0, inner])
        last = placed(cells[depth + 1, inner])
        for z in range(depth):
            for h in range(2):
                base = pl.multiple_of(s * STRIP, STRIP) + h * HALF
                part = slice(h * HALF, (h + 1) * HALF)
                here = pl.ds(base + HALF, HALF)
                value = wide[z, here]
                behind = wide[z - 1, here] if z > 0 else first[part]
                ahead = wide[z + 1, here] if z + 1 < depth else last[part]
                gz = ahead - behind
                gy = wide[z, pl.ds(base + HALF + 1, HALF)] - wide[z, pl.ds(base + HALF - 1, HALF)]
                gx = diff[pl.ds(z * STRIP + h * HALF, HALF)]
                root = lax.rsqrt(gz * gz + gy * gy + (gx * gx + square))
                lit = jnp.abs(gz + (LIGHT_Y / LIGHT_Z) * gy + (LIGHT_X / LIGHT_Z) * gx)
                shading = AMBIENT / light + lit * root
                scaled = jnp.clip(value, 0.0, knots - 1.0)
                interval = scaled.astype(jnp.int32)
                pair = lax.shift_right_logical(interval, 1)
                away = scaled - (interval | 1).astype(jnp.float32)
                red, green, blue, extinction = [
                    look_up(odd, pair, 0) + look_up(slope, interval, 1) * away for odd, slope in tables
                ]
                passed = jnp.exp2(extinction * (1.2 / square - root * root))
                after = through[h] * passed
                weight = (through[h] - after) * shading
                through[h] = after
                for channel, value_of in enumerate((red, green, blue)):
                    colour[h][channel] = colour[h][channel] + value_of * weight
        return [jnp.concatenate([colour[0][i], colour[1][i]], axis=0) for i in range(3)] + [
            jnp.concatenate(through, axis=0)
        ]

    def chip_of(i):
        ahead = jnp.where(i % 2 == 0, chips // 2 - i // 2, chips // 2 + (i + 1) // 2)
        return lax.rem(chip + ahead, chips)

    def swap(i):
        return pltpu.make_async_remote_copy(
            src_ref=parts.at[i],
            dst_ref=theirs.at[i],
            send_sem=swap_send.at[i],
            recv_sem=swap_recv.at[i],
            device_id={"view": partner},
            device_id_type=MESH,
        )

    def hand_over(to_chip, from_chip):
        return pltpu.make_async_remote_copy(
            src_ref=outgoing.at[to_chip],
            dst_ref=arrived.at[from_chip],
            send_sem=part_send.at[to_chip],
            recv_sem=part_recv.at[from_chip],
            device_id={"view": CORES * to_chip + core},
            device_id_type=MESH,
        )

    def strip_of(step):
        side = jnp.where(step < chips, 1 - core, core)
        return CORES * chip_of(lax.rem(step, chips)) + side

    diff_even[...] = difference_x(strip_of(0))

    def give(t, carry):
        for odd, diff, following in ((0, diff_even, diff_odd), (1, diff_odd, diff_even)):
            i = 2 * t + odd
            following[...] = difference_x(strip_of(i + 1))
            image = partial_image(strip_of(i), diff)
            for channel in range(4):
                parts[i, channel] = image[channel]
            swap(i).start()
        return carry

    lax.fori_loop(0, chips // 2, give, 0)

    def merge(t, carry):
        for odd in range(2):
            swap(2 * t + odd).wait_recv()
        for odd, diff, following in ((0, diff_even, diff_odd), (1, diff_odd, diff_even)):
            i = 2 * t + odd
            to_chip = chip_of(i)
            following[...] = difference_x(strip_of(lax.rem(chips + i + 1, views)))
            image = partial_image(strip_of(chips + i), diff)
            front, back = [], []
            for channel in range(4):
                other = theirs[i, channel]
                front.append(jnp.where(core == 0, image[channel], other))
                back.append(jnp.where(core == 0, other, image[channel]))
            for channel in range(3):
                outgoing[to_chip, channel] = (front[channel] + front[3] * back[channel]).astype(jnp.bfloat16)
            outgoing[to_chip, 3] = (1.0 - front[3] * back[3]).astype(jnp.bfloat16)
            if odd == 0:
                hand_over(to_chip, chip).start()
            else:

                @pl.when(to_chip != chip)
                def _():
                    hand_over(to_chip, chip).start()

        return carry

    lax.fori_loop(0, chips // 2, merge, 0)

    for i in range(6):

        @pl.when(beside[i][0])
        def _():
            copies[i].wait_send()

    for i in range(chips):
        swap(i).wait_send()

    arrived[chip] = outgoing[chip]
    image = [jnp.zeros((STRIP, LANES), jnp.float32)] * 3
    through = jnp.ones((STRIP, LANES), jnp.float32)
    for source in range(chips):

        @pl.when(chip != source)
        def _():
            hand_over(source, source).wait()

        layer = arrived[source].astype(jnp.float32)
        for channel in range(3):
            image[channel] = image[channel] + through * layer[channel]
        through = through * (1.0 - layer[3])
    for channel in range(3):
        out_ref[channel, 0] = image[channel]
    out_ref[3, 0] = 1.0 - through


def solution(mesh):
    counts = tuple(mesh.shape[axis] for axis in ("view", "row", "col"))

    def on_device(volume, tf_color, tf_opacity):
        depth, height, width = volume.shape
        views = counts[0]
        chips = views // CORES
        half, full = jnp.bfloat16, jnp.float32
        edge_rows = height * 2 * depth // LANES
        return pl.pallas_call(
            lambda *refs: kernel(counts, *refs),
            name="render",
            out_shape=jax.ShapeDtypeStruct((4, 1, height // views, width), jnp.float32),
            in_specs=[
                pl.BlockSpec(memory_space=pl.ANY),
                pl.BlockSpec(memory_space=pl.ANY),
                pl.BlockSpec(memory_space=pl.ANY),
            ],
            out_specs=pl.BlockSpec(memory_space=pltpu.VMEM),
            scratch_shapes=[
                pltpu.SMEM(tf_color.shape, full),
                pltpu.SMEM(tf_opacity.shape, full),
                pltpu.VMEM((depth + 2, height + 2 * STRIP, width), half),
                pltpu.VMEM((depth, height + 2 * HALF, width), full),
                pltpu.VMEM((edge_rows, width), half),
                pltpu.VMEM((edge_rows, width), half),
                pltpu.VMEM((edge_rows, width), half),
                pltpu.VMEM((2 * width, width), half),
                pltpu.VMEM((depth * STRIP, width), full),
                pltpu.VMEM((depth * STRIP, width), full),
                pltpu.VMEM((LANES // 2, STRIP, width), half),
                pltpu.VMEM((chips, 4, STRIP, width), full),
                pltpu.VMEM((chips, 4, STRIP, width), full),
                pltpu.VMEM((chips, 4, STRIP, width), half),
                pltpu.VMEM((chips, 4, STRIP, width), half),
                pltpu.SemaphoreType.DMA,
                pltpu.SemaphoreType.DMA((2,)),
                pltpu.SemaphoreType.REGULAR((4,)),
                pltpu.SemaphoreType.DMA((6,)),
                pltpu.SemaphoreType.DMA((6,)),
                pltpu.SemaphoreType.DMA((chips,)),
                pltpu.SemaphoreType.DMA((chips,)),
                pltpu.SemaphoreType.DMA((chips,)),
                pltpu.SemaphoreType.DMA((chips,)),
            ],
            compiler_params=pltpu.CompilerParams(collective_id=0, has_side_effects=True, vmem_limit_bytes=56 * 10**6),
        )(volume, tf_color, tf_opacity)

    return jax.shard_map(
        on_device,
        mesh=mesh,
        in_specs=(P("view", "row", "col"), P(), P()),
        out_specs=P(None, "view", "row", "col"),
        check_vma=False,
    )
```

```python
import math

import jax
import jax.numpy as jnp
from jax import lax
from jax.experimental import pallas as pl
from jax.experimental.pallas import tpu as pltpu
from jax.sharding import PartitionSpec as P

LIGHT_Z = 0.48
LIGHT_Y = 0.6
LIGHT_X = 0.64
VALUE_LOW = -3.0
VALUE_HIGH = 3.0
AMBIENT = 0.35
DIFFUSE = 0.65

MESH = pl.DeviceIdType.MESH
LANES = 128
STRIP = 16
HALF = 8
CORES = 2
TRIP = 4


def tables_of(color_ref, opacity_ref, knots, scales):
    row = lax.broadcasted_iota(jnp.int32, (HALF, LANES), 0)
    tables = []
    for channel in range(4):
        at_knot = [
            (color_ref[channel, k] if channel < 3 else opacity_ref[k]) * scales[channel] for k in range(knots)
        ]
        rise = [at_knot[k + 1] - at_knot[k] for k in range(knots - 1)] + [0.0]
        odd, below, above = [jnp.zeros((HALF, LANES), jnp.float32) for _ in range(3)]
        for j in range(knots // 2):
            odd = jnp.where(row == j, at_knot[2 * j + 1], odd)
            below = jnp.where(row == j, rise[2 * j], below)
            above = jnp.where(row == j, rise[2 * j + 1], above)
        tables.append((odd, below, above))
    return tables


def look_up(table, index, axis):
    other = 1 - axis
    dims = lax.GatherDimensionNumbers(
        offset_dims=(),
        collapsed_slice_dims=(axis,),
        start_index_map=(axis,),
        operand_batching_dims=(other,),
        start_indices_batching_dims=(other,),
    )
    mode = lax.GatherScatterMode.PROMISE_IN_BOUNDS
    return lax.gather(table, index[..., None], dims, slice_sizes=(1, 1), mode=mode)


def kernel(
    counts,
    volume,
    color_hbm,
    opacity_hbm,
    out_ref,
    color_ref,
    opacity_ref,
    cells,
    wide,
    looked,
    edges,
    edges_left,
    edges_right,
    across,
    diffs,
    picked,
    parts,
    theirs,
    outgoing,
    arrived,
    load_sem,
    table_sem,
    ready_sem,
    halo_send,
    halo_recv,
    swap_send,
    swap_recv,
    part_send,
    part_recv,
):
    views, rows, cols = counts
    chips = views // CORES
    depth, height, _ = volume.shape
    knots = color_ref.shape[1]
    groups = LANES // (2 * depth)
    group_rows = height // groups
    v, r, c = lax.axis_index("view"), lax.axis_index("row"), lax.axis_index("col")
    core, chip = lax.rem(v, CORES), v // CORES
    partner = v + 1 - 2 * core
    body = pl.ds(STRIP, height)

    load = pltpu.make_async_copy(volume, cells.at[pl.ds(1, depth), body], load_sem)
    load.start()
    loads = [
        pltpu.make_async_copy(color_hbm, color_ref, table_sem.at[0]),
        pltpu.make_async_copy(opacity_hbm, opacity_ref, table_sem.at[1]),
    ]
    for one in loads:
        one.start()

    beside = [
        (v > 0, {"view": v - 1}),
        (v < views - 1, {"view": v + 1}),
        (r > 0, {"row": r - 1}),
        (r < rows - 1, {"row": r + 1}),
        (c > 0, {"col": c - 1}),
        (c < cols - 1, {"col": c + 1}),
    ]
    barrier = pltpu.get_barrier_semaphore()
    expected = 0
    for there, where in beside:
        expected = expected + there.astype(jnp.int32)

        @pl.when(there)
        def _():
            pl.semaphore_signal(barrier, inc=1, device_id=where, device_id_type=MESH)

    def greet(semaphore, distance):
        for way in sorted({distance, chips - distance}):
            other = lax.rem(v + CORES * way, views)
            pl.semaphore_signal(semaphore, inc=1, device_id={"view": other}, device_id_type=MESH)
        return len({distance, chips - distance})

    expected = expected + greet(barrier, 1)

    group_of = lax.broadcasted_iota(jnp.int32, (groups * depth, STRIP, LANES), 0)
    lane_of = lax.broadcasted_iota(jnp.int32, (groups * depth, STRIP, LANES), 2)
    first_lane = group_of + (group_of // depth) * depth
    own = (lane_of == first_lane) | (lane_of == first_lane + depth)
    picked[...] = own.astype(jnp.float32).astype(jnp.bfloat16)

    scale = (knots - 1) / (VALUE_HIGH - VALUE_LOW)
    square = (2.0 * scale) ** 2
    light = DIFFUSE * LIGHT_Z
    scales = [light] * 3 + [-2.0 * square * math.log2(math.e) / (depth * views)]

    def placed(some):
        return some.astype(jnp.float32) * scale - VALUE_LOW * scale

    k = lax.broadcasted_iota(jnp.int32, (2 * LANES, LANES), 0)
    n = lax.broadcasted_iota(jnp.int32, (2 * LANES, LANES), 1)
    inside = k < LANES
    place = k & (2 * depth - 1)
    plus = (inside & (k == n + 1)) | ((k >= LANES) & (place >= depth) & (n == LANES - 1))
    minus = (inside & (k == n - 1)) | ((k >= LANES) & (place < depth) & (n == 0))
    across[...] = ((plus.astype(jnp.float32) - minus.astype(jnp.float32)) * scale).astype(jnp.bfloat16)

    pl.semaphore_wait(barrier, expected)

    sources = [
        volume.at[pl.ds(0, 1)],
        volume.at[pl.ds(depth - 1, 1)],
        volume.at[:, pl.ds(0, STRIP)],
        volume.at[:, pl.ds(height - STRIP, STRIP)],
        edges,
        edges,
    ]
    landings = [
        cells.at[pl.ds(depth + 1, 1), body],
        cells.at[pl.ds(0, 1), body],
        cells.at[pl.ds(1, depth), pl.ds(STRIP + height, STRIP)],
        cells.at[pl.ds(1, depth), pl.ds(0, STRIP)],
        edges_right,
        edges_left,
    ]
    copies = [
        pltpu.make_async_remote_copy(
            src_ref=sources[i],
            dst_ref=landings[i],
            send_sem=halo_send.at[i],
            recv_sem=halo_recv.at[i],
            device_id=beside[i][1],
            device_id_type=MESH,
        )
        for i in range(6)
    ]
    for i in range(4):

        @pl.when(beside[i][0])
        def _():
            copies[i].start()

    rounds = max(chips // 2 - 1, 0).bit_length()
    heard = [greet(ready_sem.at[0], 1)] if rounds > 0 else []

    for one in loads:
        one.wait()
    tables = tables_of(color_ref, opacity_ref, knots, scales)

    load.wait()

    narrow = lax.broadcasted_iota(jnp.int32, (STRIP, LANES), 1)
    from_left = (narrow & (2 * depth - 1)) < depth
    taken = jnp.where(from_left, LANES - 1, 0).astype(jnp.int16)
    for b in range(group_rows // STRIP):
        packed = jnp.zeros((STRIP, LANES), jnp.bfloat16)
        for g in range(groups):
            for z in range(depth):
                row = cells[1 + z, pl.ds(STRIP + g * group_rows + b * STRIP, STRIP)]
                packed = packed + look_up(row, taken, 1) * picked[g * depth + z]
        edges[pl.ds(b * STRIP, STRIP)] = packed
    for i in range(4, 6):

        @pl.when(beside[i][0])
        def _():
            copies[i].start()

    for k in range(1, rounds):
        pl.semaphore_wait(ready_sem.at[k - 1], heard[-1])
        heard.append(greet(ready_sem.at[k], 2**k))

    for i in range(6):

        @pl.when(jnp.logical_not(beside[i ^ 1][0]))
        def _():
            landings[i][...] = jnp.zeros(landings[i].shape, landings[i].dtype)

    def classify(s, carry):
        for z in range(depth):
            both = placed(cells[1 + z, pl.ds(pl.multiple_of(STRIP + s * STRIP, STRIP), STRIP)])
            for h in range(2):
                value = both[h * HALF : (h + 1) * HALF]
                base = pl.multiple_of(s * STRIP, STRIP) + h * HALF
                wide[z, pl.ds(base + HALF, HALF)] = value
                scaled = jnp.clip(value, 0.0, knots - 1.0)
                interval = scaled.astype(jnp.int32)
                pair = lax.shift_right_logical(interval, 1)
                away = scaled - (interval | 1).astype(jnp.float32)
                for channel, (odd, below, above) in enumerate(tables):
                    tilt = jnp.where(away < 0.0, look_up(below, pair, 0), look_up(above, pair, 0))
                    looked[channel, z, pl.ds(base, HALF)] = look_up(odd, pair, 0) + tilt * away
        return carry

    lax.fori_loop(0, height // STRIP, classify, 0)

    for i in range(6):

        @pl.when(beside[i ^ 1][0])
        def _():
            copies[i].wait_recv()

    for z in range(depth):
        wide[z, pl.ds(0, HALF)] = placed(cells[1 + z, pl.ds(0, STRIP)])[HALF:]
        wide[z, pl.ds(HALF + height, HALF)] = placed(cells[1 + z, pl.ds(STRIP + height, STRIP)])[:HALF]
    if rounds > 0:
        pl.semaphore_wait(ready_sem.at[rounds - 1], heard[-1])

    def difference_x(s):
        inner = pl.ds(pl.multiple_of(s * STRIP + STRIP, STRIP), STRIP)
        b = pl.ds(pl.multiple_of((s * STRIP) & (group_rows - 1), STRIP), STRIP)
        outside = jnp.where(from_left, edges_left[b].astype(jnp.float32), edges_right[b].astype(jnp.float32))
        mine = picked[pl.ds(lax.shift_right_logical(s * STRIP, group_rows.bit_length() - 1) * depth, depth)]
        outside = outside.astype(jnp.bfloat16)[None] * mine
        middle = cells[pl.ds(1, depth), inner]
        left_hand = jnp.concatenate(
            [middle.reshape(depth * STRIP, LANES), outside.reshape(depth * STRIP, LANES)], axis=1
        )
        return jnp.dot(left_hand, across[...], preferred_element_type=jnp.float32)

    def partial_image(s, diff):
        diff[...] = difference_x(s)
        inner = pl.ds(pl.multiple_of(s * STRIP + STRIP, STRIP), STRIP)
        colour = [[jnp.zeros((HALF, LANES), jnp.float32)] * 3 for _ in range(2)]
        through = [jnp.ones((HALF, LANES), jnp.float32) for _ in range(2)]
        first = placed(cells[0, inner])
        last = placed(cells[depth + 1, inner])
        for z in range(depth):
            for h in range(2):
                base = pl.multiple_of(s * STRIP, STRIP) + h * HALF
                part = slice(h * HALF, (h + 1) * HALF)
                here = pl.ds(base + HALF, HALF)
                behind = wide[z - 1, here] if z > 0 else first[part]
                ahead = wide[z + 1, here] if z + 1 < depth else last[part]
                gz = ahead - behind
                gy = wide[z, pl.ds(base + HALF + 1, HALF)] - wide[z, pl.ds(base + HALF - 1, HALF)]
                gx = diff[pl.ds(z * STRIP + h * HALF, HALF)]
                root = lax.rsqrt(gz * gz + gy * gy + (gx * gx + square))
                lit = jnp.abs(gz + (LIGHT_Y / LIGHT_Z) * gy + (LIGHT_X / LIGHT_Z) * gx)
                shading = AMBIENT / light + lit * root
                red, green, blue, extinction = [looked[channel, z, pl.ds(base, HALF)] for channel in range(4)]
                passed = jnp.exp2(extinction * (1.2 / square - root * root))
                after = through[h] * passed
                weight = (through[h] - after) * shading
                through[h] = after
                for channel, value_of in enumerate((red, green, blue)):
                    colour[h][channel] = colour[h][channel] + value_of * weight
        return [jnp.concatenate([colour[0][i], colour[1][i]], axis=0) for i in range(3)] + [
            jnp.concatenate(through, axis=0)
        ]

    def chip_of(t, k):
        step = t * (TRIP // 2) + (k + 1) // 2
        return (chip + chips // 2 + (step if k % 2 else -step)) & (chips - 1)

    def swap(i):
        return pltpu.make_async_remote_copy(
            src_ref=parts.at[i],
            dst_ref=theirs.at[i],
            send_sem=swap_send.at[i],
            recv_sem=swap_recv.at[i],
            device_id={"view": partner},
            device_id_type=MESH,
        )

    def hand_over(to_chip, from_chip):
        return pltpu.make_async_remote_copy(
            src_ref=outgoing.at[to_chip],
            dst_ref=arrived.at[from_chip],
            send_sem=part_send.at[to_chip],
            recv_sem=part_recv.at[from_chip],
            device_id={"view": CORES * to_chip + core},
            device_id_type=MESH,
        )

    def give(t, carry):
        for k in range(TRIP):
            i = TRIP * t + k
            image = partial_image(CORES * chip_of(t, k) + 1 - core, diffs.at[k])
            for channel in range(4):
                parts[i, channel] = image[channel]
        for k in range(TRIP):
            swap(TRIP * t + k).start()
        return carry

    lax.fori_loop(0, chips // TRIP, give, 0)

    def merge(t, carry):
        for k in range(TRIP):
            swap(TRIP * t + k).wait_recv()
        for k in range(TRIP):
            to_chip = chip_of(t, k)
            image = partial_image(CORES * to_chip + core, diffs.at[k])
            front, back = [], []
            for channel in range(4):
                other = theirs[TRIP * t + k, channel]
                front.append(jnp.where(core == 0, image[channel], other))
                back.append(jnp.where(core == 0, other, image[channel]))
            for channel in range(3):
                outgoing[to_chip, channel] = (front[channel] + front[3] * back[channel]).astype(jnp.bfloat16)
            outgoing[to_chip, 3] = (1.0 - front[3] * back[3]).astype(jnp.bfloat16)
            if k % 2:
                hand_over(chip_of(t, k - 1), chip).start()
            if k % 2 and k < TRIP - 1:
                hand_over(to_chip, chip).start()
        to_chip = chip_of(t, TRIP - 1)

        @pl.when(to_chip != chip)
        def _():
            hand_over(to_chip, chip).start()

        return carry

    lax.fori_loop(0, chips // TRIP, merge, 0)

    for i in range(6):

        @pl.when(beside[i][0])
        def _():
            copies[i].wait_send()

    for i in range(chips):
        swap(i).wait_send()

    arrived[chip] = outgoing[chip]
    image = [jnp.zeros((STRIP, LANES), jnp.float32)] * 3
    through = jnp.ones((STRIP, LANES), jnp.float32)
    for source in range(chips):

        @pl.when(chip != source)
        def _():
            hand_over(source, source).wait()

        layer = arrived[source].astype(jnp.float32)
        for channel in range(3):
            image[channel] = image[channel] + through * layer[channel]
        through = through * (1.0 - layer[3])
    for channel in range(3):
        out_ref[channel, 0] = image[channel]
    out_ref[3, 0] = 1.0 - through


def solution(mesh):
    counts = tuple(mesh.shape[axis] for axis in ("view", "row", "col"))

    def on_device(volume, tf_color, tf_opacity):
        depth, height, width = volume.shape
        views = counts[0]
        chips = views // CORES
        half, full = jnp.bfloat16, jnp.float32
        edge_rows = height * 2 * depth // LANES
        return pl.pallas_call(
            lambda *refs: kernel(counts, *refs),
            name="render",
            out_shape=jax.ShapeDtypeStruct((4, 1, height // views, width), jnp.float32),
            in_specs=[
                pl.BlockSpec(memory_space=pl.ANY),
                pl.BlockSpec(memory_space=pl.ANY),
                pl.BlockSpec(memory_space=pl.ANY),
            ],
            out_specs=pl.BlockSpec(memory_space=pltpu.VMEM),
            scratch_shapes=[
                pltpu.SMEM(tf_color.shape, full),
                pltpu.SMEM(tf_opacity.shape, full),
                pltpu.VMEM((depth + 2, height + 2 * STRIP, width), half),
                pltpu.VMEM((depth, height + 2 * HALF, width), full),
                pltpu.VMEM((4, depth, height, width), full),
                pltpu.VMEM((edge_rows, width), half),
                pltpu.VMEM((edge_rows, width), half),
                pltpu.VMEM((edge_rows, width), half),
                pltpu.VMEM((2 * width, width), half),
                pltpu.VMEM((TRIP, depth * STRIP, width), full),
                pltpu.VMEM((LANES // 2, STRIP, width), half),
                pltpu.VMEM((chips, 4, STRIP, width), full),
                pltpu.VMEM((chips, 4, STRIP, width), full),
                pltpu.VMEM((chips, 4, STRIP, width), half),
                pltpu.VMEM((chips, 4, STRIP, width), half),
                pltpu.SemaphoreType.DMA,
                pltpu.SemaphoreType.DMA((2,)),
                pltpu.SemaphoreType.REGULAR((4,)),
                pltpu.SemaphoreType.DMA((6,)),
                pltpu.SemaphoreType.DMA((6,)),
                pltpu.SemaphoreType.DMA((chips,)),
                pltpu.SemaphoreType.DMA((chips,)),
                pltpu.SemaphoreType.DMA((chips,)),
                pltpu.SemaphoreType.DMA((chips,)),
            ],
            compiler_params=pltpu.CompilerParams(collective_id=0, has_side_effects=True, vmem_limit_bytes=56 * 10**6),
        )(*[pltpu.with_memory_space_constraint(x, pltpu.HBM) for x in (volume, tf_color, tf_opacity)])

    return jax.shard_map(
        on_device,
        mesh=mesh,
        in_specs=(P("view", "row", "col"), P(), P()),
        out_specs=P(None, "view", "row", "col"),
        check_vma=False,
    )
```

```python
import math

import jax
import jax.numpy as jnp
from jax import lax
from jax.experimental import pallas as pl
from jax.experimental.pallas import tpu as pltpu
from jax.sharding import PartitionSpec as P

LIGHT_Z = 0.48
LIGHT_Y = 0.6
LIGHT_X = 0.64
VALUE_LOW = -3.0
VALUE_HIGH = 3.0
AMBIENT = 0.35
DIFFUSE = 0.65

MESH = pl.DeviceIdType.MESH
LANES = 128
STRIP = 16
HALF = 8
CORES = 2
TRIP = 4


def tables_of(color_ref, opacity_ref, knots, scales):
    row = lax.broadcasted_iota(jnp.int32, (HALF, LANES), 0)
    tables = []
    for channel in range(4):
        at_knot = [
            (color_ref[channel, k] if channel < 3 else opacity_ref[k]) * scales[channel] for k in range(knots)
        ]
        rise = [2.0 * (at_knot[k + 1] - at_knot[k]) for k in range(knots - 1)] + [0.0]
        odd, below, above = [jnp.zeros((HALF, LANES), jnp.float32) for _ in range(3)]
        for j in range(knots // 2):
            odd = jnp.where(row == j, at_knot[2 * j + 1], odd)
            below = jnp.where(row == j, rise[2 * j], below)
            above = jnp.where(row == j, rise[2 * j + 1], above)
        tables.append((odd, below, above))
    return tables


def look_up(table, index, axis):
    other = 1 - axis
    dims = lax.GatherDimensionNumbers(
        offset_dims=(),
        collapsed_slice_dims=(axis,),
        start_index_map=(axis,),
        operand_batching_dims=(other,),
        start_indices_batching_dims=(other,),
    )
    mode = lax.GatherScatterMode.PROMISE_IN_BOUNDS
    return lax.gather(table, index[..., None], dims, slice_sizes=(1, 1), mode=mode)


def kernel(
    counts,
    volume,
    color_hbm,
    opacity_hbm,
    out_ref,
    color_ref,
    opacity_ref,
    cells,
    wide,
    looked,
    edges,
    edges_left,
    edges_right,
    across,
    diffs,
    picked,
    parts,
    theirs,
    outgoing,
    arrived,
    load_sem,
    table_sem,
    ready_sem,
    halo_send,
    halo_recv,
    edge_send,
    edge_recv,
    swap_send,
    swap_recv,
    part_send,
    part_recv,
):
    views, rows, cols = counts
    chips = views // CORES
    depth, height, _ = volume.shape
    knots = color_ref.shape[1]
    trips = chips // TRIP
    v, r, c = lax.axis_index("view"), lax.axis_index("row"), lax.axis_index("col")
    core, chip = lax.rem(v, CORES), v // CORES
    partner = v + 1 - 2 * core
    body = pl.ds(STRIP, height)

    load = pltpu.make_async_copy(volume, cells.at[pl.ds(1, depth), body], load_sem)
    load.start()
    loads = [
        pltpu.make_async_copy(color_hbm, color_ref, table_sem.at[0]),
        pltpu.make_async_copy(opacity_hbm, opacity_ref, table_sem.at[1]),
    ]
    for one in loads:
        one.start()

    beside = [
        (v > 0, {"view": v - 1}),
        (v < views - 1, {"view": v + 1}),
        (r > 0, {"row": r - 1}),
        (r < rows - 1, {"row": r + 1}),
        (c > 0, {"col": c - 1}),
        (c < cols - 1, {"col": c + 1}),
    ]
    barrier = pltpu.get_barrier_semaphore()
    expected = 0
    for there, where in beside:
        expected = expected + there.astype(jnp.int32)

        @pl.when(there)
        def _():
            pl.semaphore_signal(barrier, inc=1, device_id=where, device_id_type=MESH)

    def greet(semaphore, distance):
        for way in sorted({distance, chips - distance}):
            other = lax.rem(v + CORES * way, views)
            pl.semaphore_signal(semaphore, inc=1, device_id={"view": other}, device_id_type=MESH)
        return len({distance, chips - distance})

    expected = expected + greet(barrier, 1)

    group_of = lax.broadcasted_iota(jnp.int32, (TRIP * depth, STRIP, LANES), 0)
    lane_of = lax.broadcasted_iota(jnp.int32, (TRIP * depth, STRIP, LANES), 2)
    first_lane = group_of + (group_of // depth) * depth
    own = (lane_of == first_lane) | (lane_of == first_lane + depth)
    picked[...] = own.astype(jnp.float32).astype(jnp.bfloat16)

    scale = (knots - 1) / (VALUE_HIGH - VALUE_LOW) / 2
    shift = -VALUE_LOW * scale - 0.5
    square = (2.0 * scale) ** 2
    light = DIFFUSE * LIGHT_Z
    scales = [light] * 3 + [-2.0 * square * math.log2(math.e) / (depth * views)]

    def placed(some):
        return some.astype(jnp.float32) * scale + shift

    k = lax.broadcasted_iota(jnp.int32, (2 * LANES, LANES), 0)
    n = lax.broadcasted_iota(jnp.int32, (2 * LANES, LANES), 1)
    inside = k < LANES
    place = k & (2 * depth - 1)
    plus = (inside & (k == n + 1)) | ((k >= LANES) & (place >= depth) & (n == LANES - 1))
    minus = (inside & (k == n - 1)) | ((k >= LANES) & (place < depth) & (n == 0))
    across[...] = ((plus.astype(jnp.float32) - minus.astype(jnp.float32)) * scale).astype(jnp.bfloat16)

    sources = [
        volume.at[pl.ds(0, 1)],
        volume.at[pl.ds(depth - 1, 1)],
        volume.at[:, pl.ds(0, STRIP)],
        volume.at[:, pl.ds(height - STRIP, STRIP)],
    ]
    landings = [
        cells.at[pl.ds(depth + 1, 1), body],
        cells.at[pl.ds(0, 1), body],
        cells.at[pl.ds(1, depth), pl.ds(STRIP + height, STRIP)],
        cells.at[pl.ds(1, depth), pl.ds(0, STRIP)],
        edges_right,
        edges_left,
    ]
    copies = [
        pltpu.make_async_remote_copy(
            src_ref=sources[i],
            dst_ref=landings[i],
            send_sem=halo_send.at[i],
            recv_sem=halo_recv.at[i],
            device_id=beside[i][1],
            device_id_type=MESH,
        )
        for i in range(4)
    ]

    def edge_copy(i, q):
        return pltpu.make_async_remote_copy(
            src_ref=edges.at[q],
            dst_ref=landings[i].at[q],
            send_sem=edge_send.at[i - 4, q],
            recv_sem=edge_recv.at[i - 4, q],
            device_id=beside[i][1],
            device_id_type=MESH,
        )

    for i in range(6):

        @pl.when(jnp.logical_not(beside[i ^ 1][0]))
        def _():
            landings[i][...] = jnp.zeros(landings[i].shape, landings[i].dtype)

    def chip_of(t, k):
        step = t * (TRIP // 2) + (k + 1) // 2
        return (chip + chips // 2 + (step if k % 2 else -step)) & (chips - 1)

    for one in loads:
        one.wait()
    tables = tables_of(color_ref, opacity_ref, knots, scales)
    narrow = lax.broadcasted_iota(jnp.int32, (STRIP, LANES), 1)
    from_left = (narrow & (2 * depth - 1)) < depth
    taken = jnp.where(from_left, LANES - 1, 0).astype(jnp.int16)
    rounds = max(chips // 2 - 1, 0).bit_length()
    ways = [len({2**k, chips - 2**k}) for k in range(rounds)]
    load.wait()

    def classify(q, carry):
        side = jnp.where(q < trips, 1 - core, core)
        packed = jnp.zeros((STRIP, LANES), jnp.bfloat16)
        for k in range(TRIP):
            s = CORES * chip_of(q & (trips - 1), k) + side
            for z in range(depth):
                row = cells[1 + z, pl.ds(pl.multiple_of(STRIP + s * STRIP, STRIP), STRIP)]
                packed = packed + look_up(row, taken, 1) * picked[k * depth + z]
                both = placed(row)
                for h in range(2):
                    value = both[h * HALF : (h + 1) * HALF]
                    base = pl.multiple_of(s * STRIP, STRIP) + h * HALF
                    wide[z, pl.ds(base + HALF, HALF)] = value
                    held = jnp.clip(value, -0.5, knots / 2 - 1.0)
                    nearest = jnp.round(held)
                    away = held - nearest
                    pair = nearest.astype(jnp.int32)
                    for channel, (odd, below, above) in enumerate(tables):
                        tilt = jnp.where(away < 0.0, look_up(below, pair, 0), look_up(above, pair, 0))
                        looked[channel, z, pl.ds(base, HALF)] = look_up(odd, pair, 0) + tilt * away
        edges[q] = packed

        @pl.when(q == 0)
        def _():
            pl.semaphore_wait(barrier, expected)
            for i in range(4):

                @pl.when(beside[i][0])
                def _():
                    copies[i].start()

            if rounds > 0:
                greet(ready_sem.at[0], 1)

        for k in range(1, rounds):

            @pl.when(q == k)
            def _():
                pl.semaphore_wait(ready_sem.at[k - 1], ways[k - 1])
                greet(ready_sem.at[k], 2**k)

        for i in range(4, 6):

            @pl.when(beside[i][0])
            def _():
                edge_copy(i, q).start()

        return carry

    lax.fori_loop(0, 2 * trips, classify, 0)

    for i in range(4):

        @pl.when(beside[i ^ 1][0])
        def _():
            copies[i].wait_recv()

    for z in range(depth):
        wide[z, pl.ds(0, HALF)] = placed(cells[1 + z, pl.ds(0, STRIP)])[HALF:]
        wide[z, pl.ds(HALF + height, HALF)] = placed(cells[1 + z, pl.ds(STRIP + height, STRIP)])[:HALF]

    def edges_of(q):
        for i in range(4, 6):

            @pl.when(beside[i ^ 1][0])
            def _():
                edge_copy(i, q).wait_recv()

        return jnp.where(from_left, edges_left[q].astype(jnp.float32), edges_right[q].astype(jnp.float32))

    def difference_x(s, k, beyond):
        inner = pl.ds(pl.multiple_of(s * STRIP + STRIP, STRIP), STRIP)
        outside = beyond.astype(jnp.bfloat16)[None] * picked[pl.ds(k * depth, depth)]
        middle = cells[pl.ds(1, depth), inner]
        left_hand = jnp.concatenate(
            [middle.reshape(depth * STRIP, LANES), outside.reshape(depth * STRIP, LANES)], axis=1
        )
        return jnp.dot(left_hand, across[...], preferred_element_type=jnp.float32)

    def partial_image(s, k, beyond):
        diff = diffs.at[k]
        diff[...] = difference_x(s, k, beyond)
        inner = pl.ds(pl.multiple_of(s * STRIP + STRIP, STRIP), STRIP)
        colour = [[jnp.zeros((HALF, LANES), jnp.float32)] * 3 for _ in range(2)]
        through = [jnp.ones((HALF, LANES), jnp.float32) for _ in range(2)]
        first = placed(cells[0, inner])
        last = placed(cells[depth + 1, inner])
        for z in range(depth):
            for h in range(2):
                base = pl.multiple_of(s * STRIP, STRIP) + h * HALF
                part = slice(h * HALF, (h + 1) * HALF)
                here = pl.ds(base + HALF, HALF)
                behind = wide[z - 1, here] if z > 0 else first[part]
                ahead = wide[z + 1, here] if z + 1 < depth else last[part]
                gz = ahead - behind
                gy = wide[z, pl.ds(base + HALF + 1, HALF)] - wide[z, pl.ds(base + HALF - 1, HALF)]
                gx = diff[pl.ds(z * STRIP + h * HALF, HALF)]
                root = lax.rsqrt(gz * gz + gy * gy + (gx * gx + square))
                lit = jnp.abs(gz + (LIGHT_Y / LIGHT_Z) * gy + (LIGHT_X / LIGHT_Z) * gx)
                shading = AMBIENT / light + lit * root
                red, green, blue, extinction = [looked[channel, z, pl.ds(base, HALF)] for channel in range(4)]
                passed = jnp.exp2(extinction * (1.2 / square - root * root))
                after = through[h] * passed
                weight = (through[h] - after) * shading
                through[h] = after
                for channel, value_of in enumerate((red, green, blue)):
                    colour[h][channel] = colour[h][channel] + value_of * weight
        return [jnp.concatenate([colour[0][i], colour[1][i]], axis=0) for i in range(3)] + [
            jnp.concatenate(through, axis=0)
        ]

    def swap(i):
        return pltpu.make_async_remote_copy(
            src_ref=parts.at[i],
            dst_ref=theirs.at[i],
            send_sem=swap_send.at[i],
            recv_sem=swap_recv.at[i],
            device_id={"view": partner},
            device_id_type=MESH,
        )

    def hand_over(to_chip, from_chip):
        return pltpu.make_async_remote_copy(
            src_ref=outgoing.at[to_chip],
            dst_ref=arrived.at[from_chip],
            send_sem=part_send.at[to_chip],
            recv_sem=part_recv.at[from_chip],
            device_id={"view": CORES * to_chip + core},
            device_id_type=MESH,
        )

    def give(t, carry):
        beyond = edges_of(t)
        for k in range(TRIP):
            i = TRIP * t + k
            image = partial_image(CORES * chip_of(t, k) + 1 - core, k, beyond)
            for channel in range(4):
                parts[i, channel] = image[channel]
        for k in range(TRIP):
            swap(TRIP * t + k).start()
        return carry

    lax.fori_loop(0, trips, give, 0)
    if rounds > 0:
        pl.semaphore_wait(ready_sem.at[rounds - 1], ways[-1])

    def merge(t, carry):
        beyond = edges_of(trips + t)
        for k in range(TRIP):
            swap(TRIP * t + k).wait_recv()
        for k in range(TRIP):
            to_chip = chip_of(t, k)
            image = partial_image(CORES * to_chip + core, k, beyond)
            front, back = [], []
            for channel in range(4):
                other = theirs[TRIP * t + k, channel]
                front.append(jnp.where(core == 0, image[channel], other))
                back.append(jnp.where(core == 0, other, image[channel]))
            for channel in range(3):
                outgoing[to_chip, channel] = (front[channel] + front[3] * back[channel]).astype(jnp.bfloat16)
            outgoing[to_chip, 3] = (1.0 - front[3] * back[3]).astype(jnp.bfloat16)
            if k == 1:
                hand_over(chip_of(t, 0), chip).start()
            if 0 < k < TRIP - 1:
                hand_over(to_chip, chip).start()
        to_chip = chip_of(t, TRIP - 1)

        @pl.when(to_chip != chip)
        def _():
            hand_over(to_chip, chip).start()

        return carry

    lax.fori_loop(0, trips, merge, 0)

    for i in range(6):

        @pl.when(beside[i][0])
        def _():
            if i < 4:
                copies[i].wait_send()
            else:
                for q in range(2 * trips):
                    edge_copy(i, q).wait_send()

    for i in range(chips):
        swap(i).wait_send()

    arrived[chip] = outgoing[chip]
    image = [jnp.zeros((STRIP, LANES), jnp.float32)] * 3
    through = jnp.ones((STRIP, LANES), jnp.float32)
    for source in range(chips):

        @pl.when(chip != source)
        def _():
            hand_over(source, source).wait()

        layer = arrived[source].astype(jnp.float32)
        for channel in range(3):
            image[channel] = image[channel] + through * layer[channel]
        through = through * (1.0 - layer[3])
    for channel in range(3):
        out_ref[channel, 0] = image[channel]
    out_ref[3, 0] = 1.0 - through


def solution(mesh):
    counts = tuple(mesh.shape[axis] for axis in ("view", "row", "col"))

    def on_device(volume, tf_color, tf_opacity):
        depth, height, width = volume.shape
        views = counts[0]
        chips = views // CORES
        half, full = jnp.bfloat16, jnp.float32
        tiles = height // STRIP // TRIP
        return pl.pallas_call(
            lambda *refs: kernel(counts, *refs),
            name="render",
            out_shape=jax.ShapeDtypeStruct((4, 1, height // views, width), jnp.float32),
            in_specs=[
                pl.BlockSpec(memory_space=pl.ANY),
                pl.BlockSpec(memory_space=pl.ANY),
                pl.BlockSpec(memory_space=pl.ANY),
            ],
            out_specs=pl.BlockSpec(memory_space=pltpu.VMEM),
            scratch_shapes=[
                pltpu.SMEM(tf_color.shape, full),
                pltpu.SMEM(tf_opacity.shape, full),
                pltpu.VMEM((depth + 2, height + 2 * STRIP, width), half),
                pltpu.VMEM((depth, height + 2 * HALF, width), full),
                pltpu.VMEM((4, depth, height, width), full),
                pltpu.VMEM((tiles, STRIP, width), half),
                pltpu.VMEM((tiles, STRIP, width), half),
                pltpu.VMEM((tiles, STRIP, width), half),
                pltpu.VMEM((2 * width, width), half),
                pltpu.VMEM((TRIP, depth * STRIP, width), full),
                pltpu.VMEM((TRIP * depth, STRIP, width), half),
                pltpu.VMEM((chips, 4, STRIP, width), full),
                pltpu.VMEM((chips, 4, STRIP, width), full),
                pltpu.VMEM((chips, 4, STRIP, width), half),
                pltpu.VMEM((chips, 4, STRIP, width), half),
                pltpu.SemaphoreType.DMA,
                pltpu.SemaphoreType.DMA((2,)),
                pltpu.SemaphoreType.REGULAR((4,)),
                pltpu.SemaphoreType.DMA((4,)),
                pltpu.SemaphoreType.DMA((4,)),
                pltpu.SemaphoreType.DMA((2, tiles)),
                pltpu.SemaphoreType.DMA((2, tiles)),
                pltpu.SemaphoreType.DMA((chips,)),
                pltpu.SemaphoreType.DMA((chips,)),
                pltpu.SemaphoreType.DMA((chips,)),
                pltpu.SemaphoreType.DMA((chips,)),
            ],
            compiler_params=pltpu.CompilerParams(collective_id=0, has_side_effects=True, vmem_limit_bytes=56 * 10**6),
        )(*[pltpu.with_memory_space_constraint(x, pltpu.HBM) for x in (volume, tf_color, tf_opacity)])

    return jax.shard_map(
        on_device,
        mesh=mesh,
        in_specs=(P("view", "row", "col"), P(), P()),
        out_specs=P(None, "view", "row", "col"),
        check_vma=False,
    )
```

```python
import math

import jax
import jax.numpy as jnp
from jax import lax
from jax.experimental import pallas as pl
from jax.experimental.pallas import tpu as pltpu
from jax.sharding import PartitionSpec as P

LIGHT_Z = 0.48
LIGHT_Y = 0.6
LIGHT_X = 0.64
VALUE_LOW = -3.0
VALUE_HIGH = 3.0
AMBIENT = 0.35
DIFFUSE = 0.65

MESH = pl.DeviceIdType.MESH
LANES = 128
STRIP = 16
HALF = 8
CORES = 2
TRIP = 4


def tables_of(color_ref, opacity_ref, knots, scales):
    row = lax.broadcasted_iota(jnp.int32, (HALF, LANES), 0)
    tables = []
    for channel in range(4):
        at_knot = [
            (color_ref[channel, k] if channel < 3 else opacity_ref[k]) * scales[channel] for k in range(knots)
        ]
        rise = [2.0 * (at_knot[k + 1] - at_knot[k]) for k in range(knots - 1)] + [0.0]
        odd, below, above = [jnp.zeros((HALF, LANES), jnp.float32) for _ in range(3)]
        for j in range(knots // 2):
            odd = jnp.where(row == j, at_knot[2 * j + 1], odd)
            below = jnp.where(row == j, rise[2 * j], below)
            above = jnp.where(row == j, rise[2 * j + 1], above)
        tables.append((odd, below, above))
    return tables


def look_up(table, index, axis):
    other = 1 - axis
    dims = lax.GatherDimensionNumbers(
        offset_dims=(),
        collapsed_slice_dims=(axis,),
        start_index_map=(axis,),
        operand_batching_dims=(other,),
        start_indices_batching_dims=(other,),
    )
    mode = lax.GatherScatterMode.PROMISE_IN_BOUNDS
    return lax.gather(table, index[..., None], dims, slice_sizes=(1, 1), mode=mode)


def kernel(
    counts,
    volume,
    color_hbm,
    opacity_hbm,
    out_ref,
    color_ref,
    opacity_ref,
    cells,
    wide,
    looked,
    edges,
    edges_left,
    edges_right,
    across,
    diffs,
    picked,
    parts,
    theirs,
    outgoing,
    arrived,
    load_sem,
    table_sem,
    ready_sem,
    halo_send,
    halo_recv,
    edge_send,
    edge_recv,
    swap_send,
    swap_recv,
    part_send,
    part_recv,
):
    views, rows, cols = counts
    chips = views // CORES
    depth, height, _ = volume.shape
    knots = color_ref.shape[1]
    trips = chips // TRIP
    v, r, c = lax.axis_index("view"), lax.axis_index("row"), lax.axis_index("col")
    core, chip = lax.rem(v, CORES), v // CORES
    partner = v + 1 - 2 * core
    body = pl.ds(STRIP, height)

    load = pltpu.make_async_copy(volume, cells.at[pl.ds(1, depth), body], load_sem)
    load.start()
    loads = [
        pltpu.make_async_copy(color_hbm, color_ref, table_sem.at[0]),
        pltpu.make_async_copy(opacity_hbm, opacity_ref, table_sem.at[1]),
    ]
    for one in loads:
        one.start()

    beside = [
        (v > 0, {"view": v - 1}),
        (v < views - 1, {"view": v + 1}),
        (r > 0, {"row": r - 1}),
        (r < rows - 1, {"row": r + 1}),
        (c > 0, {"col": c - 1}),
        (c < cols - 1, {"col": c + 1}),
    ]
    barrier = pltpu.get_barrier_semaphore()
    expected = 0
    for there, where in beside:
        expected = expected + there.astype(jnp.int32)

        @pl.when(there)
        def _():
            pl.semaphore_signal(barrier, inc=1, device_id=where, device_id_type=MESH)

    def greet(semaphore, distance):
        for way in sorted({distance, chips - distance}):
            other = lax.rem(v + CORES * way, views)
            pl.semaphore_signal(semaphore, inc=1, device_id={"view": other}, device_id_type=MESH)
        return len({distance, chips - distance})

    expected = expected + greet(barrier, 1)

    group_of = lax.broadcasted_iota(jnp.int32, (TRIP * depth, STRIP, LANES), 0)
    lane_of = lax.broadcasted_iota(jnp.int32, (TRIP * depth, STRIP, LANES), 2)
    first_lane = group_of + (group_of // depth) * depth
    own = (lane_of == first_lane) | (lane_of == first_lane + depth)
    picked[...] = own.astype(jnp.float32).astype(jnp.bfloat16)

    scale = (knots - 1) / (VALUE_HIGH - VALUE_LOW) / 2
    shift = -VALUE_LOW * scale - 0.5
    square = (2.0 * scale) ** 2
    light = DIFFUSE * LIGHT_Z
    scales = [light] * 3 + [-2.0 * square * math.log2(math.e) / (depth * views)]

    def placed(some):
        return some.astype(jnp.float32) * scale + shift

    k = lax.broadcasted_iota(jnp.int32, (2 * LANES, LANES), 0)
    n = lax.broadcasted_iota(jnp.int32, (2 * LANES, LANES), 1)
    inside = k < LANES
    place = k & (2 * depth - 1)
    plus = (inside & (k == n + 1)) | ((k >= LANES) & (place >= depth) & (n == LANES - 1))
    minus = (inside & (k == n - 1)) | ((k >= LANES) & (place < depth) & (n == 0))
    across[...] = ((plus.astype(jnp.float32) - minus.astype(jnp.float32)) * scale).astype(jnp.bfloat16)

    sources = [
        volume.at[pl.ds(0, 1)],
        volume.at[pl.ds(depth - 1, 1)],
        volume.at[:, pl.ds(0, STRIP)],
        volume.at[:, pl.ds(height - STRIP, STRIP)],
    ]
    landings = [
        cells.at[pl.ds(depth + 1, 1), body],
        cells.at[pl.ds(0, 1), body],
        cells.at[pl.ds(1, depth), pl.ds(STRIP + height, STRIP)],
        cells.at[pl.ds(1, depth), pl.ds(0, STRIP)],
        edges_right,
        edges_left,
    ]
    copies = [
        pltpu.make_async_remote_copy(
            src_ref=sources[i],
            dst_ref=landings[i],
            send_sem=halo_send.at[i],
            recv_sem=halo_recv.at[i],
            device_id=beside[i][1],
            device_id_type=MESH,
        )
        for i in range(4)
    ]

    def edge_copy(i, q):
        return pltpu.make_async_remote_copy(
            src_ref=edges.at[q],
            dst_ref=landings[i].at[q],
            send_sem=edge_send.at[i - 4, q],
            recv_sem=edge_recv.at[i - 4, q],
            device_id=beside[i][1],
            device_id_type=MESH,
        )

    for i in range(6):

        @pl.when(jnp.logical_not(beside[i ^ 1][0]))
        def _():
            landings[i][...] = jnp.zeros(landings[i].shape, landings[i].dtype)

    def chip_of(t, k):
        step = t * (TRIP // 2) + (k + 1) // 2
        return (chip + chips // 2 + (step if k % 2 else -step)) & (chips - 1)

    for one in loads:
        one.wait()
    tables = tables_of(color_ref, opacity_ref, knots, scales)
    narrow = lax.broadcasted_iota(jnp.int32, (STRIP, LANES), 1)
    from_left = (narrow & (2 * depth - 1)) < depth
    taken = jnp.where(from_left, LANES - 1, 0).astype(jnp.int16)
    rounds = max(chips // 2 - 1, 0).bit_length()
    ways = [len({2**k, chips - 2**k}) for k in range(rounds)]
    pl.semaphore_wait(barrier, expected)
    for i in range(4):

        @pl.when(beside[i][0])
        def _():
            copies[i].start()

    if rounds > 0:
        greet(ready_sem.at[0], 1)
    load.wait()

    def classify(q, carry):
        side = jnp.where(q < trips, 1 - core, core)
        packed = jnp.zeros((STRIP, LANES), jnp.bfloat16)
        for k in range(TRIP):
            s = CORES * chip_of(q & (trips - 1), k) + side
            for z in range(depth):
                row = cells[1 + z, pl.ds(pl.multiple_of(STRIP + s * STRIP, STRIP), STRIP)]
                packed = packed + look_up(row, taken, 1) * picked[k * depth + z]
                both = placed(row)
                for h in range(2):
                    value = both[h * HALF : (h + 1) * HALF]
                    base = pl.multiple_of(s * STRIP, STRIP) + h * HALF
                    wide[z, pl.ds(base + HALF, HALF)] = value
                    held = jnp.clip(value, -0.5, knots / 2 - 1.0)
                    nearest = jnp.round(held)
                    away = held - nearest
                    pair = nearest.astype(jnp.int32)
                    for channel, (odd, below, above) in enumerate(tables):
                        tilt = jnp.where(away < 0.0, look_up(below, pair, 0), look_up(above, pair, 0))
                        looked[channel, z, pl.ds(base, HALF)] = look_up(odd, pair, 0) + tilt * away
        edges[q] = packed

        for k in range(1, rounds):

            @pl.when(q == k)
            def _():
                pl.semaphore_wait(ready_sem.at[k - 1], ways[k - 1])
                greet(ready_sem.at[k], 2**k)

        for i in range(4, 6):

            @pl.when(beside[i][0])
            def _():
                edge_copy(i, q).start()

        return carry

    lax.fori_loop(0, 2 * trips, classify, 0)

    for i in range(4):

        @pl.when(beside[i ^ 1][0])
        def _():
            copies[i].wait_recv()

    for z in range(depth):
        wide[z, pl.ds(0, HALF)] = placed(cells[1 + z, pl.ds(0, STRIP)])[HALF:]
        wide[z, pl.ds(HALF + height, HALF)] = placed(cells[1 + z, pl.ds(STRIP + height, STRIP)])[:HALF]

    def edges_of(q):
        for i in range(4, 6):

            @pl.when(beside[i ^ 1][0])
            def _():
                edge_copy(i, q).wait_recv()

        return jnp.where(from_left, edges_left[q].astype(jnp.float32), edges_right[q].astype(jnp.float32))

    def difference_x(s, k, beyond):
        inner = pl.ds(pl.multiple_of(s * STRIP + STRIP, STRIP), STRIP)
        outside = beyond.astype(jnp.bfloat16)[None] * picked[pl.ds(k * depth, depth)]
        middle = cells[pl.ds(1, depth), inner]
        left_hand = jnp.concatenate(
            [middle.reshape(depth * STRIP, LANES), outside.reshape(depth * STRIP, LANES)], axis=1
        )
        return jnp.dot(left_hand, across[...], preferred_element_type=jnp.float32)

    def partial_image(s, k, beyond):
        diff = diffs.at[k]
        diff[...] = difference_x(s, k, beyond)
        inner = pl.ds(pl.multiple_of(s * STRIP + STRIP, STRIP), STRIP)
        colour = [[jnp.zeros((HALF, LANES), jnp.float32)] * 3 for _ in range(2)]
        through = [jnp.ones((HALF, LANES), jnp.float32) for _ in range(2)]
        first = placed(cells[0, inner])
        last = placed(cells[depth + 1, inner])
        for z in range(depth):
            for h in range(2):
                base = pl.multiple_of(s * STRIP, STRIP) + h * HALF
                part = slice(h * HALF, (h + 1) * HALF)
                here = pl.ds(base + HALF, HALF)
                behind = wide[z - 1, here] if z > 0 else first[part]
                ahead = wide[z + 1, here] if z + 1 < depth else last[part]
                gz = ahead - behind
                gy = wide[z, pl.ds(base + HALF + 1, HALF)] - wide[z, pl.ds(base + HALF - 1, HALF)]
                gx = diff[pl.ds(z * STRIP + h * HALF, HALF)]
                root = lax.rsqrt(gz * gz + gy * gy + (gx * gx + square))
                lit = jnp.abs(gz + (LIGHT_Y / LIGHT_Z) * gy + (LIGHT_X / LIGHT_Z) * gx)
                shading = AMBIENT / light + lit * root
                red, green, blue, extinction = [looked[channel, z, pl.ds(base, HALF)] for channel in range(4)]
                passed = jnp.exp2(extinction * (1.2 / square - root * root))
                after = through[h] * passed
                weight = (through[h] - after) * shading
                through[h] = after
                for channel, value_of in enumerate((red, green, blue)):
                    colour[h][channel] = colour[h][channel] + value_of * weight
        return [jnp.concatenate([colour[0][i], colour[1][i]], axis=0) for i in range(3)] + [
            jnp.concatenate(through, axis=0)
        ]

    def swap(i):
        return pltpu.make_async_remote_copy(
            src_ref=parts.at[i],
            dst_ref=theirs.at[i],
            send_sem=swap_send.at[i],
            recv_sem=swap_recv.at[i],
            device_id={"view": partner},
            device_id_type=MESH,
        )

    def hand_over(to_chip, from_chip):
        return pltpu.make_async_remote_copy(
            src_ref=outgoing.at[to_chip],
            dst_ref=arrived.at[from_chip],
            send_sem=part_send.at[to_chip],
            recv_sem=part_recv.at[from_chip],
            device_id={"view": CORES * to_chip + core},
            device_id_type=MESH,
        )

    def give(t, carry):
        beyond = edges_of(t)
        for k in range(TRIP):
            i = TRIP * t + k
            image = partial_image(CORES * chip_of(t, k) + 1 - core, k, beyond)
            for channel in range(4):
                parts[i, channel] = image[channel]
        for k in range(TRIP):
            swap(TRIP * t + k).start()
        return carry

    lax.fori_loop(0, trips, give, 0)
    if rounds > 0:
        pl.semaphore_wait(ready_sem.at[rounds - 1], ways[-1])

    def merge(t, carry):
        beyond = edges_of(trips + t)
        for k in range(TRIP):
            swap(TRIP * t + k).wait_recv()
        for k in range(TRIP):
            to_chip = chip_of(t, k)
            image = partial_image(CORES * to_chip + core, k, beyond)
            front, back = [], []
            for channel in range(4):
                other = theirs[TRIP * t + k, channel]
                front.append(jnp.where(core == 0, image[channel], other))
                back.append(jnp.where(core == 0, other, image[channel]))
            for channel in range(3):
                outgoing[to_chip, channel] = (front[channel] + front[3] * back[channel]).astype(jnp.bfloat16)
            outgoing[to_chip, 3] = (1.0 - front[3] * back[3]).astype(jnp.bfloat16)
            if k == 1:
                hand_over(chip_of(t, 0), chip).start()
            if 0 < k < TRIP - 1:
                hand_over(to_chip, chip).start()
        to_chip = chip_of(t, TRIP - 1)

        @pl.when(to_chip != chip)
        def _():
            hand_over(to_chip, chip).start()

        return carry

    lax.fori_loop(0, trips, merge, 0)

    for i in range(6):

        @pl.when(beside[i][0])
        def _():
            if i < 4:
                copies[i].wait_send()
            else:
                for q in range(2 * trips):
                    edge_copy(i, q).wait_send()

    for i in range(chips):
        swap(i).wait_send()

    arrived[chip] = outgoing[chip]
    image = [jnp.zeros((STRIP, LANES), jnp.float32)] * 3
    through = jnp.ones((STRIP, LANES), jnp.float32)
    for source in range(chips):

        @pl.when(chip != source)
        def _():
            hand_over(source, source).wait()

        layer = arrived[source].astype(jnp.float32)
        for channel in range(3):
            image[channel] = image[channel] + through * layer[channel]
        through = through * (1.0 - layer[3])
    for channel in range(3):
        out_ref[channel, 0] = image[channel]
    out_ref[3, 0] = 1.0 - through


def solution(mesh):
    counts = tuple(mesh.shape[axis] for axis in ("view", "row", "col"))

    def on_device(volume, tf_color, tf_opacity):
        depth, height, width = volume.shape
        views = counts[0]
        chips = views // CORES
        half, full = jnp.bfloat16, jnp.float32
        tiles = height // STRIP // TRIP
        return pl.pallas_call(
            lambda *refs: kernel(counts, *refs),
            name="render",
            out_shape=jax.ShapeDtypeStruct((4, 1, height // views, width), jnp.float32),
            in_specs=[
                pl.BlockSpec(memory_space=pl.ANY),
                pl.BlockSpec(memory_space=pl.ANY),
                pl.BlockSpec(memory_space=pl.ANY),
            ],
            out_specs=pl.BlockSpec(memory_space=pltpu.VMEM),
            scratch_shapes=[
                pltpu.SMEM(tf_color.shape, full),
                pltpu.SMEM(tf_opacity.shape, full),
                pltpu.VMEM((depth + 2, height + 2 * STRIP, width), half),
                pltpu.VMEM((depth, height + 2 * HALF, width), full),
                pltpu.VMEM((4, depth, height, width), full),
                pltpu.VMEM((tiles, STRIP, width), half),
                pltpu.VMEM((tiles, STRIP, width), half),
                pltpu.VMEM((tiles, STRIP, width), half),
                pltpu.VMEM((2 * width, width), half),
                pltpu.VMEM((TRIP, depth * STRIP, width), full),
                pltpu.VMEM((TRIP * depth, STRIP, width), half),
                pltpu.VMEM((chips, 4, STRIP, width), full),
                pltpu.VMEM((chips, 4, STRIP, width), full),
                pltpu.VMEM((chips, 4, STRIP, width), half),
                pltpu.VMEM((chips, 4, STRIP, width), half),
                pltpu.SemaphoreType.DMA,
                pltpu.SemaphoreType.DMA((2,)),
                pltpu.SemaphoreType.REGULAR((4,)),
                pltpu.SemaphoreType.DMA((4,)),
                pltpu.SemaphoreType.DMA((4,)),
                pltpu.SemaphoreType.DMA((2, tiles)),
                pltpu.SemaphoreType.DMA((2, tiles)),
                pltpu.SemaphoreType.DMA((chips,)),
                pltpu.SemaphoreType.DMA((chips,)),
                pltpu.SemaphoreType.DMA((chips,)),
                pltpu.SemaphoreType.DMA((chips,)),
            ],
            compiler_params=pltpu.CompilerParams(collective_id=0, has_side_effects=True, vmem_limit_bytes=56 * 10**6),
        )(*[pltpu.with_memory_space_constraint(x, pltpu.HBM) for x in (volume, tf_color, tf_opacity)])

    return jax.shard_map(
        on_device,
        mesh=mesh,
        in_specs=(P("view", "row", "col"), P(), P()),
        out_specs=P(None, "view", "row", "col"),
        check_vma=False,
    )
```
